32 devices in a mesh: blk: 4 (over y, x), team: 4 (over z), dp: 2 (over core).
Axes of the slice: x: 2, y: 2, z: 4, core: 2. Of those that a mesh axis runs over, the one named last changes fastest.
Arguments:
- hidden: bfloat16 [1024, 28672], P(('blk', 'dp'), 'team'), may hold values from -6 to 6
- out_grad: bfloat16 [1024, 8192], P(('blk', 'dp'), 'team'), may hold values from -0.1875 to 0.1875
- act_rows: int32 [4, 64, 12], P('team'), may hold values from 0 to 55, as said below
- col_owner: int32 [64], replicated, may hold values from 0 to 3, as said below
Outputs:
- gradients: float32 [4, 4, 288, 128, 128], P('team', 'blk', 'dp')
- scores: float32 [4, 4, 288], P('team', 'blk', 'dp')
The draws below stay inside these ranges and needn't reach their ends.
Inputs may be any that keep to these rules, and one draw needn't show every extreme that they name: For each t and c the 12 entries act_rows[t, c, :] are distinct. `col_owner`: some owner holds exactly 24 block columns and no owner holds more.
All inputs are finite; a program needn't handle non-finite values.
Results may differ from the reference program's by a relative error of at most 0.0003.
Values may be sent and summed in bfloat16 or wider, within the bound.
A program may use at most 192 MiB of HBM per device.

```python
import jax
import jax.numpy as jnp
from jax import lax

D = 8192
FF = 28672
BS = 128
KC = 12
DB = 64
FBT = 56
CAPC = 24
CAP = 288
TOKENS = 1024
N_BLK = 4
N_TEAM = 4


def draw_act_rows(key, part):
    key_list = jax.random.split(key, N_TEAM * DB)
    chosen = jax.vmap(lambda subkey: jax.random.permutation(subkey, FBT)[:KC])(key_list)
    return chosen.reshape(N_TEAM, DB, KC).astype(jnp.int32)


def draw_col_owner(key, part):
    first_key, second_key = jax.random.split(jax.random.fold_in(key, 7))
    shuffle = jax.random.permutation(first_key, DB)
    busiest = jax.random.randint(second_key, (), 0, N_BLK)
    position = jnp.arange(DB, dtype=jnp.int32)
    others = (position - CAPC) % (N_BLK - 1)
    others = others + (others >= busiest).astype(jnp.int32)
    values = jnp.where(position < CAPC, busiest, others).astype(jnp.int32)
    return jnp.zeros((DB,), jnp.int32).at[shuffle].set(values)


def block_levels(stream_key, shape, cuts, smallest, top_value):
    factor_of, own = 1.0, jax.random.fold_in(stream_key, 6)
    for axis_at, parts in cuts:
        heights = jnp.exp(jax.random.uniform(jax.random.fold_in(own, axis_at), (parts,), jnp.float32, smallest / len(cuts), top_value / len(cuts)))
        factor_of = factor_of * jnp.repeat(heights, shape[axis_at] // parts).reshape([-1 if axis == axis_at else 1 for axis in range(len(shape))])
    return factor_of


def centred(rng, dims, spread, bound, shards=(), kind=jnp.bfloat16):
    loudness = block_levels(rng, dims, shards, -0.22, 0.18) if shards else 1.0
    array = jax.random.normal(rng, dims, jnp.float32) * spread * loudness
    return jnp.minimum(jnp.maximum(array, -bound), bound).astype(kind)


def setup_inputs(seed: int = 0) -> dict:
    seeds = jax.random.split(jax.random.key(seed), 5)
    hidden = centred(seeds[0], (TOKENS, FF), 1.0, 6.0, ((0, 8), (1, 4)))
    out_grad = centred(seeds[1], (TOKENS, D), (TOKENS ** -0.5), 0.1875, ((0, 8), (1, 4)))
    act_rows = draw_act_rows(jax.random.fold_in(seeds[4], 71), 0)
    col_owner = draw_col_owner(jax.random.fold_in(seeds[4], 71), 0)
    return {"hidden": hidden, "out_grad": out_grad, "act_rows": act_rows, "col_owner": col_owner}


epsilon = 1e-06

def owner_tables(col_owner):
    owners = jnp.arange(N_BLK, dtype=jnp.int32)
    onehot = (col_owner[:, None] == owners[None, :]).astype(jnp.int32)
    column_rank = lax.optimization_barrier(jnp.sum((jnp.cumsum(onehot, axis=0) - onehot) * onehot, axis=1))
    slot_ids = jnp.arange(CAPC, dtype=jnp.int32)
    matches = (col_owner[None, None, :] == owners[:, None, None]) & (column_rank[None, None, :] == slot_ids[None, :, None])
    owned_columns = lax.optimization_barrier(jnp.sum(matches.astype(jnp.int32) * jnp.arange(DB, dtype=jnp.int32)[None, None, :], axis=2))
    alive_mask = jnp.any(matches, axis=2)
    return (owned_columns, alive_mask)

def reference(hidden, out_grad, act_rows, col_owner):
    owned_columns, alive_mask = owner_tables(col_owner)
    team_width = FF // N_TEAM
    grad_blocks = out_grad.reshape(TOKENS, DB, BS)

    def one_owner(position):
        team_index = position // N_BLK
        owner_index = position % N_BLK
        team_hidden = lax.dynamic_slice_in_dim(hidden, (team_index * team_width).astype(jnp.int32), team_width, 1)
        team_hidden = team_hidden.reshape(TOKENS, FBT, BS)
        chosen = owned_columns[owner_index]
        living = alive_mask[owner_index]
        block_rows = act_rows[team_index][chosen]
        picked_hidden = jnp.take(team_hidden, block_rows.reshape(-1), axis=1).reshape(TOKENS, CAPC, KC, BS).astype(jnp.float32)
        picked_grad = jnp.take(grad_blocks, chosen, axis=1).astype(jnp.float32)
        blocks = jnp.einsum('ncki,ncj->ckij', picked_hidden, picked_grad)
        blocks = blocks * living.astype(jnp.float32)[:, None, None, None]
        return blocks.reshape(CAP, BS, BS)
    gradients = lax.map(one_owner, jnp.arange(N_TEAM * N_BLK, dtype=jnp.int32))
    gradients = gradients.reshape(N_TEAM, N_BLK, CAP, BS, BS)
    scores = jnp.sqrt(lax.optimization_barrier(jnp.mean(gradients * gradients, axis=(3, 4))) + epsilon)
    return (gradients, scores)
```

```python
import jax
import jax.numpy as jnp
from jax import lax
from jax.experimental import pallas as pl
from jax.experimental.pallas import tpu as pltpu
from jax.sharding import PartitionSpec as P

BS = 128
MESH = pl.DeviceIdType.MESH
HALVES = 2
GROUP = 4


epsilon = 1e-06


def owner_tables(col_owner, owners_count, capacity):
    column_blocks = col_owner.shape[0]
    owners = jnp.arange(owners_count, dtype=jnp.int32)
    onehot = (col_owner[:, None] == owners[None, :]).astype(jnp.int32)
    column_rank = jnp.sum((jnp.cumsum(onehot, axis=0) - onehot) * onehot, axis=1)
    slot_ids = jnp.arange(capacity, dtype=jnp.int32)
    matches = (col_owner[None, None, :] == owners[:, None, None]) & (
        column_rank[None, None, :] == slot_ids[None, :, None]
    )
    owned_all = jnp.sum(
        matches.astype(jnp.int32) * jnp.arange(column_blocks, dtype=jnp.int32)[None, None, :],
        axis=2,
    )
    return owned_all, jnp.any(matches, axis=2)


def shard_of(i, t, teams):
    paired = 2 * jnp.minimum(t, teams - 1 - t)
    step = (i + 1) // 2
    near = t - step if i % 2 else t + step
    far = jnp.where(2 * t < teams, i, teams - 1 - i)
    return jnp.where(i <= paired, near, far)


def columns_of(slot, rows_ref, first, count):
    return [
        slot[:, pl.ds(rows_ref[first + i] * BS, BS)] for i in range(count)
    ]


def products(slot, rows_ref, first, count, g):
    return lax.dot_general(
        jnp.concatenate(columns_of(slot, rows_ref, first, count), axis=1),
        g,
        (((0,), (0,)), ((), ())),
        preferred_element_type=jnp.float32,
    ).reshape(count, BS, BS)


def gather_kernel(cols_ref, rows_ref, hid_ref, grad_ref, last_ref, gfull, acc, *scratch):
    *slots, gz, gcol, snd, send_sem, recv_sem, local_sem = scratch
    slots = [*slots, last_ref]
    teams = lax.axis_size("team")
    b, t, d = lax.axis_index("blk"), lax.axis_index("team"), lax.axis_index("dp")
    y, x = b // 2, b % 2
    panels, picks = cols_ref.shape
    per_column = rows_ref.shape[0] // picks
    part_rows = hid_ref.shape[0] // teams
    half_rows = part_rows // HALVES
    part_cols = grad_ref.shape[1]

    def plane(sy, sx, sd):
        oy = 1 - y if sy else y
        ox = 1 - x if sx else x
        return oy * 2 + ox, (1 - d if sd else d)

    def panel_of(sy, sx, sd):
        ob, od = plane(sy, sx, sd)
        return ob * 2 + od

    def device(sy, sx, sd):
        ob, od = plane(sy, sx, sd)
        return (ob, t, od)

    mine = panel_of(0, 0, 0)
    flips = [(sy, sx, sd) for sy in (0, 1) for sx in (0, 1) for sd in (0, 1)][1:]

    barrier = pltpu.get_barrier_semaphore()
    for flip in flips:
        pl.semaphore_signal(barrier, inc=1, device_id=device(*flip), device_id_type=MESH)
    for s in range(1, teams):
        pl.semaphore_signal(
            barrier, inc=1, device_id=(b, (t + s) % teams, d), device_id_type=MESH
        )
    pl.semaphore_wait(barrier, len(flips) + teams - 1)

    counter = [0, 0]
    sent, local = [], []

    def remote(src, dst, target, slot=None):
        started = slot is None
        if started:
            slot = counter[0]
            counter[0] += 1
        copy = pltpu.make_async_remote_copy(
            src_ref=src,
            dst_ref=dst,
            send_sem=send_sem.at[slot],
            recv_sem=recv_sem.at[slot],
            device_id=target,
            device_id_type=MESH,
        )
        if started:
            copy.start()
            sent.append(copy)
        return copy

    def within(src, dst):
        copy = pltpu.make_async_copy(src, dst, local_sem.at[counter[1]])
        counter[1] += 1
        copy.start()
        return copy

    X, Y, SIB = (0, 1, 0), (1, 0, 0), (0, 0, 1)
    panel_x, panel_y, panel_xy = panel_of(*X), panel_of(*Y), panel_of(1, 1, 0)

    def part(k, half):
        return pl.ds(k * part_rows + half * half_rows, half_rows)

    def place(panel, half):
        return pl.ds((half * panels + panel) * half_rows, half_rows)

    shards = [shard_of(i, t, teams) for i in range(teams)]

    def send_own(flip, i, half):
        return remote(
            hid_ref.at[part(shards[i], half)], slots[i].at[place(mine, half)], device(*flip)
        )

    def forward(panel, flip, i, half):
        piece = slots[i].at[place(panel, half)]
        return remote(piece, piece, device(*flip))

    from_x, from_y, from_xy = {}, {}, {}
    from_sib = [[] for _ in range(teams)]
    own_hidden = [[] for _ in range(teams)]

    def start_own(i):
        from_x[i, 0] = send_own(X, i, 0)
        from_y[i, 1] = send_own(Y, i, 1)
        from_x[i, 1] = send_own(X, i, 1)
        from_y[i, 0] = send_own(Y, i, 0)
        for half in range(HALVES):
            from_sib[i].append(send_own(SIB, i, half))
            own_hidden[i].append(
                within(hid_ref.at[part(shards[i], half)], slots[i].at[place(mine, half)])
            )

    def sibling(panel, i, half):
        from_sib[i].append(forward(panel, SIB, i, half))

    def turn(i):
        from_x[i, 0].wait_recv()
        from_xy[i, 0] = forward(panel_x, Y, i, 0)
        from_y[i, 1].wait_recv()
        from_xy[i, 1] = forward(panel_y, X, i, 1)
        sibling(panel_x, i, 0)
        sibling(panel_y, i, 1)

    def rest(i):
        from_x[i, 1].wait_recv()
        sibling(panel_x, i, 1)
        from_y[i, 0].wait_recv()
        sibling(panel_y, i, 0)

    def corner(i):
        for half in range(HALVES):
            from_xy[i, half].wait_recv()
            sibling(panel_xy, i, half)

    def arrived(i):
        for copy in from_sib[i]:
            copy.wait_recv()
        for copy in own_hidden[i]:
            copy.wait()

    def held(half):
        return pl.ds(half * half_rows, half_rows)

    def quarter(k):
        return pl.ds(k * part_cols, part_cols)

    own_grad, stage1, own_pick, stage2 = [], [], [], []
    for half in range(HALVES):
        for s in range(1, teams):
            target = (t + s) % teams
            stage1.append(
                remote(
                    grad_ref.at[part(target, half)],
                    gz.at[held(half), quarter(t)],
                    (b, target, d),
                )
            )
        own_grad.append(within(grad_ref.at[part(t, half)], gz.at[held(half), quarter(t)]))

    def pick_columns(half):
        own_grad[half].wait()
        for copy in stage1[half * (teams - 1) : (half + 1) * (teams - 1)]:
            copy.wait_recv()
        rows = slice(half * half_rows, (half + 1) * half_rows)
        for c in range(gcol.shape[1]):
            gcol[half, c] = gz[rows, c * BS : (c + 1) * BS]

        def pick(p, carry):
            for j in range(picks):
                snd[half, p, :, j * BS : (j + 1) * BS] = gcol[half, cols_ref[p, j]]
            return carry

        lax.fori_loop(0, panels, pick, 0)
        landing = gfull.at[t, place(mine, half)]
        for flip in flips:
            stage2.append(remote(snd.at[half, panel_of(*flip)], landing, device(*flip)))
        own_pick.append(within(snd.at[half, mine], landing))

    def picked(half):
        own_pick[half].wait()
        for copy in stage2[half * len(flips) : (half + 1) * len(flips)]:
            copy.wait_recv()

    chain_base = send_sem.shape[0] - 2 * (teams - 1) * HALVES
    chain_rows = panels * half_rows

    def chain(up, k, shard, target, half):
        piece = gfull.at[shard, pl.ds(half * chain_rows, chain_rows)]
        step = k if up else teams - 1 + k
        return remote(piece, piece, (b, target, d), chain_base + step * HALVES + half)

    def chain_send(k, half, wait):
        @pl.when((t < teams - 1) & (t - k >= 0))
        def _():
            copy = chain(True, k, t - k, t + 1, half)
            copy.wait_send() if wait else copy.start()

        @pl.when((t > 0) & (t + k < teams))
        def _():
            copy = chain(False, k, t + k, t - 1, half)
            copy.wait_send() if wait else copy.start()

    def chain_step(k, half):
        @pl.when(t - 1 - k >= 0)
        def _():
            chain(True, k, t - 1 - k, t - 1, half).wait_recv()

        @pl.when(t + 1 + k < teams)
        def _():
            chain(False, k, t + 1 + k, t + 1, half).wait_recv()

        if k < teams - 2:
            chain_send(k + 1, half, False)

    def accumulate(i, lo, hi):
        def column(j, carry):
            g = gfull[shards[i], :, pl.ds(pl.multiple_of(j * BS, BS), BS)]
            for k in range(0, per_column, GROUP):
                first = j * per_column + k
                block = products(slots[i], rows_ref, first, GROUP, g)
                at = pl.ds(first, GROUP)
                acc[at] = block if i == 0 else acc[at] + block
            return carry

        lax.fori_loop(lo, hi, column, 0)

    middle = picks // 2
    start_own(0)
    pick_columns(0)
    turn(0)
    pick_columns(1)
    for i in range(teams):
        if i:
            turn(i)
        if i + 1 < teams:
            start_own(i + 1)
        if i == 0:
            picked(0)
            chain_send(0, 0, False)
            rest(0)
            corner(0)
            picked(1)
            chain_send(0, 1, False)
        else:
            chain_step(i - 1, 0)
            accumulate(i - 1, middle, picks)
            rest(i)
            chain_step(i - 1, 1)
            corner(i)
        arrived(i)
        if i + 1 < teams:
            accumulate(i, 0, middle)
    for copy in sent:
        copy.wait_send()
    for k in range(teams - 1):
        for half in range(HALVES):
            chain_send(k, half, True)


def gather(columns, rows, hidden, out_grad):
    teams = lax.axis_size("team")
    panel_rows, units = hidden.shape
    panels, picks = columns.shape
    part_rows = panel_rows // teams
    half_rows = part_rows // HALVES
    group = panels * part_rows
    copies = (3 * (teams - 1) + panels - 1) * HALVES + 7 * HALVES * teams
    locals_ = HALVES * (2 + teams)
    hbm = pl.BlockSpec(memory_space=pl.ANY)
    smem = pl.BlockSpec(memory_space=pltpu.SMEM)
    vmem = pl.BlockSpec(memory_space=pltpu.VMEM)
    return pl.pallas_call(
        gather_kernel,
        out_shape=(
            pltpu.VMEM((group, units), hidden.dtype),
            pltpu.VMEM((teams, group, picks * BS), out_grad.dtype),
            pltpu.VMEM((rows.shape[0], BS, BS), jnp.float32),
        ),
        in_specs=[smem, smem, hbm, hbm],
        out_specs=(vmem, vmem, vmem),
        scratch_shapes=[pltpu.VMEM((group, units), hidden.dtype)] * (teams - 1)
        + [
            pltpu.VMEM((part_rows, teams * out_grad.shape[1]), out_grad.dtype),
            pltpu.VMEM(
                (HALVES, teams * out_grad.shape[1] // BS, half_rows, BS), out_grad.dtype
            ),
            pltpu.VMEM((HALVES, panels, half_rows, picks * BS), out_grad.dtype),
            pltpu.SemaphoreType.DMA((copies,)),
            pltpu.SemaphoreType.DMA((copies,)),
            pltpu.SemaphoreType.DMA((locals_,)),
        ],
        compiler_params=pltpu.CompilerParams(
            collective_id=0, has_side_effects=True, vmem_limit_bytes=24 << 20
        ),
    )(columns, rows, hidden, out_grad)


def finish_kernel(rows_ref, alive_ref, h_ref, g_ref, acc_ref, out_ref, score_ref, ssq):
    j = pl.program_id(0)
    picks = pl.num_programs(0)
    per_column = out_ref.shape[0]
    teams = g_ref.shape[0]
    shard = shard_of(teams - 1, lax.axis_index("team"), teams)
    scale = alive_ref[j].astype(jnp.float32)
    g = g_ref[shard, :, pl.ds(pl.multiple_of(j * BS, BS), BS)]

    @pl.when(j == 0)
    def _():
        ssq[...] = jnp.zeros_like(ssq)

    for k in range(0, per_column, GROUP):
        first = j * per_column + k
        block = acc_ref[pl.ds(first, GROUP)] + products(h_ref, rows_ref, first, GROUP, g)
        block = block * scale
        out_ref[k : k + GROUP] = block
        ssq[pl.ds(first, GROUP), :] = jnp.sum(block * block, axis=1)

    @pl.when(j == picks - 1)
    def _():
        total = jnp.sum(ssq[...].T, axis=0, keepdims=True)
        scores = jnp.sqrt(total * (1.0 / (BS * BS)) + epsilon)
        score_ref[...] = scores[:, : score_ref.shape[1]]


def finish(rows, alive, last, grad, acc):
    picks = alive.shape[0]
    slots = rows.shape[0]
    per_column = slots // picks
    vmem = pl.BlockSpec(memory_space=pltpu.VMEM)
    return pl.pallas_call(
        finish_kernel,
        out_shape=(
            jax.ShapeDtypeStruct((slots, BS, BS), jnp.float32),
            jax.ShapeDtypeStruct((1, slots), jnp.float32),
        ),
        grid_spec=pltpu.PrefetchScalarGridSpec(
            num_scalar_prefetch=2,
            grid=(picks,),
            in_specs=[vmem, vmem, vmem],
            out_specs=(
                pl.BlockSpec((per_column, BS, BS), lambda j, *_: (j, 0, 0)),
                pl.BlockSpec((1, slots), lambda j, *_: (0, 0)),
            ),
            scratch_shapes=[pltpu.VMEM((pl.cdiv(slots, BS) * BS, BS), jnp.float32)],
        ),
        compiler_params=pltpu.CompilerParams(
            dimension_semantics=("arbitrary",), vmem_limit_bytes=12 << 20
        ),
    )(rows, alive, last, grad, acc)


def in_plane(hidden, out_grad, act_rows, col_owner):
    owners_count, cores = lax.axis_size("blk"), lax.axis_size("dp")
    column_blocks = col_owner.shape[0]
    capacity = min(3 * column_blocks // (2 * owners_count), 3 * column_blocks // 4)
    owned_all, alive_all = owner_tables(col_owner, owners_count, capacity)
    panels = owners_count * cores
    picks = capacity // cores
    columns = owned_all.reshape(panels, picks)
    mine = lax.axis_index("blk") * cores + lax.axis_index("dp")
    columns_mine = lax.dynamic_index_in_dim(columns, mine, 0, keepdims=False)
    alive_mine = lax.dynamic_index_in_dim(
        alive_all.reshape(panels, picks), mine, 0, keepdims=False
    ).astype(jnp.int32)
    rows = jnp.take(act_rows[0], columns_mine, axis=0).reshape(-1)
    last, grad, acc = gather(columns, rows, hidden, out_grad)
    gradients, scores = finish(rows, alive_mine, last, grad, acc)
    return (gradients[None, None], scores[None])


def on_device(hidden, out_grad, act_rows, col_owner):
    owners_count = lax.axis_size("blk")
    owner_index = lax.axis_index("blk")
    column_blocks = col_owner.shape[0]
    capacity = min(3 * column_blocks // (2 * owners_count), 3 * column_blocks // 4)
    per_column = act_rows.shape[2]
    owned_all, alive_all = owner_tables(col_owner, owners_count, capacity)
    owned_mine = lax.dynamic_index_in_dim(owned_all, owner_index, 0, keepdims=False)
    alive_mine = lax.dynamic_index_in_dim(alive_all, owner_index, 0, keepdims=False)
    block_rows = jnp.take(act_rows[0], owned_mine, axis=0).reshape(-1)
    grad_full = lax.all_gather(out_grad, "team", axis=1, tiled=True)
    grad_mask = alive_mine.astype(jnp.bfloat16)[None, :, None]
    hidden_piece = lax.all_gather(hidden, "blk", axis=0, tiled=True)
    grad_piece = lax.all_gather(grad_full, "blk", axis=0, tiled=True)
    count_rows = grad_piece.shape[0]
    picked_grad = (
        jnp.take(grad_piece.reshape(count_rows, column_blocks, BS), owned_mine, axis=1) * grad_mask
    )
    hidden_blocks = hidden_piece.reshape(count_rows, -1, BS)
    picked_hidden = jnp.take(hidden_blocks, block_rows, axis=1).reshape(
        count_rows, capacity, per_column, BS
    )
    partial_value = jnp.einsum(
        "ncki,ncj->ckij", picked_hidden, picked_grad, preferred_element_type=jnp.float32
    )
    partial_value = partial_value.reshape(capacity * per_column, BS, BS)
    gradients = lax.psum_scatter(partial_value, "dp", scatter_dimension=0, tiled=True)
    scores = jnp.sqrt(jnp.mean(gradients * gradients, axis=(1, 2)) + epsilon)
    return (gradients[None, None], scores[None, None])


def solution(mesh):
    in_specs = (P(("blk", "dp"), "team"), P(("blk", "dp"), "team"), P("team", None, None), P())
    out_specs = (P("team", "blk", "dp", None, None), P("team", "blk", "dp"))
    square = mesh.shape["blk"] == 4 and mesh.shape["dp"] == 2
    return jax.shard_map(
        in_plane if square else on_device,
        mesh=mesh,
        in_specs=in_specs,
        out_specs=out_specs,
        check_vma=False,
    )
```

```python
import jax
import jax.numpy as jnp
from jax import lax
from jax.experimental import pallas as pl
from jax.experimental.pallas import tpu as pltpu
from jax.sharding import PartitionSpec as P

BS = 128
MESH = pl.DeviceIdType.MESH
HALVES = 2
GROUP = 4


epsilon = 1e-06


def owner_tables(col_owner, owners_count, capacity):
    column_blocks = col_owner.shape[0]
    owners = jnp.arange(owners_count, dtype=jnp.int32)
    onehot = (col_owner[:, None] == owners[None, :]).astype(jnp.int32)
    column_rank = jnp.sum((jnp.cumsum(onehot, axis=0) - onehot) * onehot, axis=1)
    slot_ids = jnp.arange(capacity, dtype=jnp.int32)
    matches = (col_owner[None, None, :] == owners[:, None, None]) & (
        column_rank[None, None, :] == slot_ids[None, :, None]
    )
    owned_all = jnp.sum(
        matches.astype(jnp.int32) * jnp.arange(column_blocks, dtype=jnp.int32)[None, None, :],
        axis=2,
    )
    return owned_all, jnp.any(matches, axis=2)


def shard_of(i, t, teams):
    paired = 2 * jnp.minimum(t, teams - 1 - t)
    step = (i + 1) // 2
    near = t - step if i % 2 else t + step
    far = jnp.where(2 * t < teams, i, teams - 1 - i)
    return jnp.where(i <= paired, near, far)


def columns_of(slot, rows_ref, first, count):
    return [
        slot[:, pl.ds(rows_ref[first + i] * BS, BS)] for i in range(count)
    ]


def products(slot, rows_ref, first, count, g):
    return lax.dot_general(
        jnp.concatenate(columns_of(slot, rows_ref, first, count), axis=1),
        g,
        (((0,), (0,)), ((), ())),
        preferred_element_type=jnp.float32,
    ).reshape(count, BS, BS)


def gather_kernel(
    owner_ref, act_ref, hid_ref, grad_ref, last_ref, gfull, acc, rows_ref, *scratch
):
    *slots, gz, gcol, snd, owner, act, cols_row, cols, send_sem, recv_sem, local_sem = scratch
    slots = [*slots, last_ref]
    teams = lax.axis_size("team")
    b, t, d = lax.axis_index("blk"), lax.axis_index("team"), lax.axis_index("dp")
    y, x = b // 2, b % 2
    _, panels, _, width = snd.shape
    picks = width // BS
    per_column = rows_ref.shape[0] // picks
    column_blocks = owner.shape[0]
    owners_count = lax.axis_size("blk")
    capacity = panels * picks // owners_count
    part_rows = hid_ref.shape[0] // teams
    half_rows = part_rows // HALVES
    part_cols = grad_ref.shape[1]

    def plane(sy, sx, sd):
        oy = 1 - y if sy else y
        ox = 1 - x if sx else x
        return oy * 2 + ox, (1 - d if sd else d)

    def panel_of(sy, sx, sd):
        ob, od = plane(sy, sx, sd)
        return ob * 2 + od

    def device(sy, sx, sd):
        ob, od = plane(sy, sx, sd)
        return (ob, t, od)

    mine = panel_of(0, 0, 0)
    flips = [(sy, sx, sd) for sy in (0, 1) for sx in (0, 1) for sd in (0, 1)][1:]

    barrier = pltpu.get_barrier_semaphore()
    for flip in flips:
        pl.semaphore_signal(barrier, inc=1, device_id=device(*flip), device_id_type=MESH)
    for s in range(1, teams):
        pl.semaphore_signal(
            barrier, inc=1, device_id=(b, (t + s) % teams, d), device_id_type=MESH
        )
    pl.semaphore_wait(barrier, len(flips) + teams - 1)

    counter = [0, 0]
    sent, local = [], []

    def remote(src, dst, target, slot=None):
        started = slot is None
        if started:
            slot = counter[0]
            counter[0] += 1
        copy = pltpu.make_async_remote_copy(
            src_ref=src,
            dst_ref=dst,
            send_sem=send_sem.at[slot],
            recv_sem=recv_sem.at[slot],
            device_id=target,
            device_id_type=MESH,
        )
        if started:
            copy.start()
            sent.append(copy)
        return copy

    def within(src, dst):
        copy = pltpu.make_async_copy(src, dst, local_sem.at[counter[1]])
        counter[1] += 1
        copy.start()
        return copy

    X, Y, SIB = (0, 1, 0), (1, 0, 0), (0, 0, 1)
    panel_x, panel_y, panel_xy = panel_of(*X), panel_of(*Y), panel_of(1, 1, 0)

    def part(k, half):
        return pl.ds(k * part_rows + half * half_rows, half_rows)

    def place(panel, half):
        return pl.ds((half * panels + panel) * half_rows, half_rows)

    shards = [shard_of(i, t, teams) for i in range(teams)]

    def send_own(flip, i, half):
        return remote(
            hid_ref.at[part(shards[i], half)], slots[i].at[place(mine, half)], device(*flip)
        )

    def forward(panel, flip, i, half):
        piece = slots[i].at[place(panel, half)]
        return remote(piece, piece, device(*flip))

    from_x, from_y, from_xy = {}, {}, {}
    from_sib = [[] for _ in range(teams)]
    own_hidden = [[] for _ in range(teams)]

    def start_own(i):
        from_x[i, 0] = send_own(X, i, 0)
        from_y[i, 1] = send_own(Y, i, 1)
        from_x[i, 1] = send_own(X, i, 1)
        from_y[i, 0] = send_own(Y, i, 0)
        for half in range(HALVES):
            from_sib[i].append(send_own(SIB, i, half))
            own_hidden[i].append(
                within(hid_ref.at[part(shards[i], half)], slots[i].at[place(mine, half)])
            )

    def sibling(panel, i, half):
        from_sib[i].append(forward(panel, SIB, i, half))

    def turn(i):
        from_x[i, 0].wait_recv()
        from_xy[i, 0] = forward(panel_x, Y, i, 0)
        from_y[i, 1].wait_recv()
        from_xy[i, 1] = forward(panel_y, X, i, 1)
        sibling(panel_x, i, 0)
        sibling(panel_y, i, 1)

    def rest(i):
        from_x[i, 1].wait_recv()
        sibling(panel_x, i, 1)
        from_y[i, 0].wait_recv()
        sibling(panel_y, i, 0)

    def corner(i):
        for half in range(HALVES):
            from_xy[i, half].wait_recv()
            sibling(panel_xy, i, half)

    def arrived(i):
        for copy in from_sib[i]:
            copy.wait_recv()
        for copy in own_hidden[i]:
            copy.wait()

    def held(half):
        return pl.ds(half * half_rows, half_rows)

    def quarter(k):
        return pl.ds(k * part_cols, part_cols)

    own_grad, stage1, own_pick, stage2 = [], [], [], []
    for half in range(HALVES):
        for s in range(1, teams):
            target = (t + s) % teams
            stage1.append(
                remote(
                    grad_ref.at[part(target, half)],
                    gz.at[held(half), quarter(t)],
                    (b, target, d),
                )
            )
        own_grad.append(within(grad_ref.at[part(t, half)], gz.at[held(half), quarter(t)]))

    def fetch_tables():
        return [within(owner_ref, owner), within(act_ref, act)]

    def own_columns():
        lanes = lax.broadcasted_iota(jnp.int32, cols_row.shape, 1)
        row = jnp.full(cols_row.shape, column_blocks, jnp.int32)
        ranks = [jnp.int32(k * capacity) for k in range(owners_count)]
        for c in range(column_blocks):
            slot = ranks[0]
            holds = [owner[c] == k for k in range(owners_count)]
            for k in range(1, owners_count):
                slot = jnp.where(holds[k], ranks[k], slot)
            row = jnp.where(lanes == slot, c, row)
            ranks = [jnp.where(holds[k], ranks[k] + 1, ranks[k]) for k in range(owners_count)]
        cols_row[...] = row

    def own_rows():
        def column(j, carry):
            c = jnp.minimum(cols[0, mine * picks + j], column_blocks - 1)
            for k in range(per_column):
                rows_ref[j * per_column + k] = act[k, 0, c]
            return carry

        lax.fori_loop(0, picks, column, 0)

    def pick_columns(half):
        own_grad[half].wait()
        for copy in stage1[half * (teams - 1) : (half + 1) * (teams - 1)]:
            copy.wait_recv()
        rows = slice(half * half_rows, (half + 1) * half_rows)
        for c in range(column_blocks):
            gcol[half, c] = gz[rows, c * BS : (c + 1) * BS]
        gcol[half, column_blocks] = jnp.zeros(gcol.shape[2:], gcol.dtype)

        def pick(p, carry):
            for j in range(picks):
                snd[half, p, :, j * BS : (j + 1) * BS] = gcol[half, cols[0, p * picks + j]]
            return carry

        lax.fori_loop(0, panels, pick, 0)
        landing = gfull.at[t, place(mine, half)]
        for flip in flips:
            stage2.append(remote(snd.at[half, panel_of(*flip)], landing, device(*flip)))
        own_pick.append(within(snd.at[half, mine], landing))

    def picked(half):
        own_pick[half].wait()
        for copy in stage2[half * len(flips) : (half + 1) * len(flips)]:
            copy.wait_recv()

    chain_base = send_sem.shape[0] - 2 * (teams - 1) * HALVES
    chain_rows = panels * half_rows

    def chain(up, k, shard, target, half):
        piece = gfull.at[shard, pl.ds(half * chain_rows, chain_rows)]
        step = k if up else teams - 1 + k
        return remote(piece, piece, (b, target, d), chain_base + step * HALVES + half)

    def chain_send(k, half, wait):
        @pl.when((t < teams - 1) & (t - k >= 0))
        def _():
            copy = chain(True, k, t - k, t + 1, half)
            copy.wait_send() if wait else copy.start()

        @pl.when((t > 0) & (t + k < teams))
        def _():
            copy = chain(False, k, t + k, t - 1, half)
            copy.wait_send() if wait else copy.start()

    def chain_step(k, half):
        @pl.when(t - 1 - k >= 0)
        def _():
            chain(True, k, t - 1 - k, t - 1, half).wait_recv()

        @pl.when(t + 1 + k < teams)
        def _():
            chain(False, k, t + 1 + k, t + 1, half).wait_recv()

        if k < teams - 2:
            chain_send(k + 1, half, False)

    def accumulate(i, lo, hi):
        def column(j, carry):
            g = gfull[shards[i], :, pl.ds(pl.multiple_of(j * BS, BS), BS)]
            for k in range(0, per_column, GROUP):
                first = j * per_column + k
                block = products(slots[i], rows_ref, first, GROUP, g)
                at = pl.ds(first, GROUP)
                acc[at] = block if i == 0 else acc[at] + block
            return carry

        lax.fori_loop(lo, hi, column, 0)

    middle = picks // 2
    tables = fetch_tables()
    start_own(0)
    for copy in tables:
        copy.wait()
    own_columns()
    moved = within(cols_row, cols)
    moved.wait()
    pick_columns(0)
    turn(0)
    pick_columns(1)
    for i in range(teams):
        if i:
            turn(i)
        if i + 1 < teams:
            start_own(i + 1)
        if i == 0:
            picked(0)
            chain_send(0, 0, False)
            rest(0)
            own_rows()
            corner(0)
            picked(1)
            chain_send(0, 1, False)
        else:
            chain_step(i - 1, 0)
            accumulate(i - 1, middle, picks)
            rest(i)
            chain_step(i - 1, 1)
            corner(i)
        arrived(i)
        if i + 1 < teams:
            accumulate(i, 0, middle)
    for copy in sent:
        copy.wait_send()
    for k in range(teams - 1):
        for half in range(HALVES):
            chain_send(k, half, True)


def gather(col_owner, act_rows, hidden, out_grad, panels, picks):
    teams = lax.axis_size("team")
    panel_rows, units = hidden.shape
    per_column = act_rows.shape[0]
    part_rows = panel_rows // teams
    half_rows = part_rows // HALVES
    group = panels * part_rows
    column_blocks = col_owner.shape[0]
    lanes = pl.cdiv(panels * picks, BS) * BS
    copies = (3 * (teams - 1) + panels - 1) * HALVES + 7 * HALVES * teams
    operands = (col_owner, act_rows, hidden, out_grad)
    hbm = pl.BlockSpec(memory_space=pltpu.HBM)
    smem = pl.BlockSpec(memory_space=pltpu.SMEM)
    vmem = pl.BlockSpec(memory_space=pltpu.VMEM)
    return pl.pallas_call(
        gather_kernel,
        out_shape=(
            pltpu.VMEM((group, units), hidden.dtype),
            pltpu.VMEM((teams, group, picks * BS), out_grad.dtype),
            pltpu.VMEM((picks * per_column, BS, BS), jnp.float32),
            pltpu.SMEM((picks * per_column,), jnp.int32),
        ),
        in_specs=[hbm] * 4,
        out_specs=(vmem, vmem, vmem, smem),
        scratch_shapes=[pltpu.VMEM((group, units), hidden.dtype)] * (teams - 1)
        + [
            pltpu.VMEM((part_rows, column_blocks * BS), out_grad.dtype),
            pltpu.VMEM((HALVES, column_blocks + 1, half_rows, BS), out_grad.dtype),
            pltpu.VMEM((HALVES, panels, half_rows, picks * BS), out_grad.dtype),
            pltpu.SMEM(col_owner.shape, jnp.int32),
            pltpu.SMEM(act_rows.shape, jnp.int32),
            pltpu.VMEM((1, lanes), jnp.int32),
            pltpu.SMEM((1, lanes), jnp.int32),
            pltpu.SemaphoreType.DMA((copies,)),
            pltpu.SemaphoreType.DMA((copies,)),
            pltpu.SemaphoreType.DMA((HALVES * (2 + teams) + 3,)),
        ],
        compiler_params=pltpu.CompilerParams(
            collective_id=0, has_side_effects=True, vmem_limit_bytes=24 << 20
        ),
    )(*(pltpu.with_memory_space_constraint(x, pltpu.HBM) for x in operands))


def finish_kernel(rows_ref, h_ref, g_ref, acc_ref, out_ref, score_ref, buf, ssq, row, sem):
    teams = g_ref.shape[0]
    picks = g_ref.shape[2] // BS
    slots = buf.shape[0]
    per_column = slots // picks
    shard = shard_of(teams - 1, lax.axis_index("team"), teams)
    ssq[slots:] = jnp.zeros((ssq.shape[0] - slots, BS), jnp.float32)
    copies = []
    for j in range(picks):
        g = g_ref[shard, :, j * BS : (j + 1) * BS]
        for first in range(j * per_column, (j + 1) * per_column, GROUP):
            at = slice(first, first + GROUP)
            block = acc_ref[at] + products(h_ref, rows_ref, first, GROUP, g)
            buf[at] = block
            ssq[at, :] = jnp.sum(block * block, axis=1)
        done = pl.ds(j * per_column, per_column)
        copies.append(pltpu.make_async_copy(buf.at[done], out_ref.at[done], sem.at[j]))
        copies[j].start()
    total = jnp.sum(ssq[...].T, axis=0, keepdims=True)
    scores = jnp.sqrt(total * (1.0 / (BS * BS)) + epsilon)
    row[...] = scores[:, :slots]
    copies.append(pltpu.make_async_copy(row, score_ref, sem.at[picks]))
    copies[picks].start()
    for copy in copies:
        copy.wait()


def finish(rows, last, grad, acc):
    slots = rows.shape[0]
    picks = grad.shape[2] // BS
    hbm = pl.BlockSpec(memory_space=pltpu.HBM)
    smem = pl.BlockSpec(memory_space=pltpu.SMEM)
    vmem = pl.BlockSpec(memory_space=pltpu.VMEM)
    return pl.pallas_call(
        finish_kernel,
        out_shape=(
            jax.ShapeDtypeStruct((slots, BS, BS), jnp.float32),
            jax.ShapeDtypeStruct((1, slots), jnp.float32),
        ),
        in_specs=[smem, vmem, vmem, vmem],
        out_specs=(hbm, hbm),
        scratch_shapes=[
            pltpu.VMEM((slots, BS, BS), jnp.float32),
            pltpu.VMEM((pl.cdiv(slots, BS) * BS, BS), jnp.float32),
            pltpu.VMEM((1, slots), jnp.float32),
            pltpu.SemaphoreType.DMA((picks + 1,)),
        ],
        compiler_params=pltpu.CompilerParams(vmem_limit_bytes=20 << 20),
    )(rows, last, grad, acc)


def in_plane(hidden, out_grad, act_rows, col_owner):
    owners_count, cores = lax.axis_size("blk"), lax.axis_size("dp")
    column_blocks = col_owner.shape[0]
    capacity = min(3 * column_blocks // (2 * owners_count), 3 * column_blocks // 4)
    last, grad, acc, rows = gather(
        col_owner,
        jnp.transpose(act_rows, (2, 0, 1)),
        hidden,
        out_grad,
        owners_count * cores,
        capacity // cores,
    )
    gradients, scores = finish(rows, last, grad, acc)
    return (gradients[None, None], scores[None])


def on_device(hidden, out_grad, act_rows, col_owner):
    owners_count = lax.axis_size("blk")
    owner_index = lax.axis_index("blk")
    column_blocks = col_owner.shape[0]
    capacity = min(3 * column_blocks // (2 * owners_count), 3 * column_blocks // 4)
    per_column = act_rows.shape[2]
    owned_all, alive_all = owner_tables(col_owner, owners_count, capacity)
    owned_mine = lax.dynamic_index_in_dim(owned_all, owner_index, 0, keepdims=False)
    alive_mine = lax.dynamic_index_in_dim(alive_all, owner_index, 0, keepdims=False)
    block_rows = jnp.take(act_rows[0], owned_mine, axis=0).reshape(-1)
    grad_full = lax.all_gather(out_grad, "team", axis=1, tiled=True)
    grad_mask = alive_mine.astype(jnp.bfloat16)[None, :, None]
    hidden_piece = lax.all_gather(hidden, "blk", axis=0, tiled=True)
    grad_piece = lax.all_gather(grad_full, "blk", axis=0, tiled=True)
    count_rows = grad_piece.shape[0]
    picked_grad = (
        jnp.take(grad_piece.reshape(count_rows, column_blocks, BS), owned_mine, axis=1) * grad_mask
    )
    hidden_blocks = hidden_piece.reshape(count_rows, -1, BS)
    picked_hidden = jnp.take(hidden_blocks, block_rows, axis=1).reshape(
        count_rows, capacity, per_column, BS
    )
    partial_value = jnp.einsum(
        "ncki,ncj->ckij", picked_hidden, picked_grad, preferred_element_type=jnp.float32
    )
    partial_value = partial_value.reshape(capacity * per_column, BS, BS)
    gradients = lax.psum_scatter(partial_value, "dp", scatter_dimension=0, tiled=True)
    scores = jnp.sqrt(jnp.mean(gradients * gradients, axis=(1, 2)) + epsilon)
    return (gradients[None, None], scores[None, None])


def solution(mesh):
    in_specs = (P(("blk", "dp"), "team"), P(("blk", "dp"), "team"), P("team", None, None), P())
    out_specs = (P("team", "blk", "dp", None, None), P("team", "blk", "dp"))
    square = mesh.shape["blk"] == 4 and mesh.shape["dp"] == 2
    return jax.shard_map(
        in_plane if square else on_device,
        mesh=mesh,
        in_specs=in_specs,
        out_specs=out_specs,
        check_vma=False,
    )
```

```python
import jax
import jax.numpy as jnp
from jax import lax
from jax.experimental import pallas as pl
from jax.experimental.pallas import tpu as pltpu
from jax.sharding import PartitionSpec as P

BS = 128
MESH = pl.DeviceIdType.MESH
HALVES = 2
PIECES = 4
GROUP = 4


epsilon = 1e-06


def owner_tables(col_owner, owners_count, capacity):
    column_blocks = col_owner.shape[0]
    owners = jnp.arange(owners_count, dtype=jnp.int32)
    onehot = (col_owner[:, None] == owners[None, :]).astype(jnp.int32)
    column_rank = jnp.sum((jnp.cumsum(onehot, axis=0) - onehot) * onehot, axis=1)
    slot_ids = jnp.arange(capacity, dtype=jnp.int32)
    matches = (col_owner[None, None, :] == owners[:, None, None]) & (
        column_rank[None, None, :] == slot_ids[None, :, None]
    )
    owned_all = jnp.sum(
        matches.astype(jnp.int32) * jnp.arange(column_blocks, dtype=jnp.int32)[None, None, :],
        axis=2,
    )
    return owned_all, jnp.any(matches, axis=2)


def shard_of(i, t, teams):
    paired = 2 * jnp.minimum(t, teams - 1 - t)
    step = (i + 1) // 2
    near = t - step if i % 2 else t + step
    far = jnp.where(2 * t < teams, i, teams - 1 - i)
    return jnp.where(i <= paired, near, far)


def columns_of(slot, rows_ref, first, count):
    return [
        slot[:, pl.ds(rows_ref[first + i] * BS, BS)] for i in range(count)
    ]


def products(slot, rows_ref, first, count, g):
    return lax.dot_general(
        jnp.concatenate(columns_of(slot, rows_ref, first, count), axis=1),
        g,
        (((0,), (0,)), ((), ())),
        preferred_element_type=jnp.float32,
    ).reshape(count, BS, BS)


def gather_kernel(
    owner_ref, act_ref, hid_ref, grad_ref, last_ref, gfull, acc, rows_ref, *scratch
):
    *slots, gz, gcol, snd, owner, act, cols_row, cols, ready, send_sem, recv_sem, local_sem = scratch
    slots = [*slots, last_ref]
    teams = lax.axis_size("team")
    b, t, d = lax.axis_index("blk"), lax.axis_index("team"), lax.axis_index("dp")
    y, x = b // 2, b % 2
    _, panels, _, width = snd.shape
    picks = width // BS
    per_column = rows_ref.shape[0] // picks
    column_blocks = owner.shape[0]
    owners_count = lax.axis_size("blk")
    capacity = panels * picks // owners_count
    part_rows = hid_ref.shape[0] // teams
    half_rows = part_rows // HALVES
    part_cols = grad_ref.shape[1]

    def plane(sy, sx, sd):
        oy = 1 - y if sy else y
        ox = 1 - x if sx else x
        return oy * 2 + ox, (1 - d if sd else d)

    def panel_of(sy, sx, sd):
        ob, od = plane(sy, sx, sd)
        return ob * 2 + od

    def device(sy, sx, sd):
        ob, od = plane(sy, sx, sd)
        return (ob, t, od)

    mine = panel_of(0, 0, 0)
    flips = [(sy, sx, sd) for sy in (0, 1) for sx in (0, 1) for sd in (0, 1)][1:]

    barrier = pltpu.get_barrier_semaphore()
    X, Y, SIB = (0, 1, 0), (1, 0, 0), (0, 0, 1)
    below, above = (t > 0).astype(jnp.int32), (t < teams - 1).astype(jnp.int32)

    def greet(sem):
        for flip in (X, Y, SIB):
            pl.semaphore_signal(sem, inc=1, device_id=device(*flip), device_id_type=MESH)

        @pl.when(t > 0)
        def _():
            pl.semaphore_signal(sem, inc=1, device_id=(b, t - 1, d), device_id_type=MESH)

        @pl.when(t < teams - 1)
        def _():
            pl.semaphore_signal(sem, inc=1, device_id=(b, t + 1, d), device_id_type=MESH)

    def met(sem):
        pl.semaphore_wait(sem, 3 + below + above)

    greet(barrier)
    met(barrier)
    greet(ready.at[0])

    counter = [0, 0]
    sent, local = [], []

    def remote(src, dst, target, slot=None):
        started = slot is None
        if started:
            slot = counter[0]
            counter[0] += 1
        copy = pltpu.make_async_remote_copy(
            src_ref=src,
            dst_ref=dst,
            send_sem=send_sem.at[slot],
            recv_sem=recv_sem.at[slot],
            device_id=target,
            device_id_type=MESH,
        )
        if started:
            copy.start()
            sent.append(copy)
        return copy

    def within(src, dst):
        copy = pltpu.make_async_copy(src, dst, local_sem.at[counter[1]])
        counter[1] += 1
        copy.start()
        return copy

    panel_x, panel_y, panel_xy = panel_of(*X), panel_of(*Y), panel_of(1, 1, 0)

    def part(k, half):
        return pl.ds(k * part_rows + half * half_rows, half_rows)

    def place(panel, half):
        return pl.ds((half * panels + panel) * half_rows, half_rows)

    shards = [shard_of(i, t, teams) for i in range(teams)]

    def send_own(flip, i, half):
        return remote(
            hid_ref.at[part(shards[i], half)], slots[i].at[place(mine, half)], device(*flip)
        )

    def forward(panel, flip, i, half):
        piece = slots[i].at[place(panel, half)]
        return remote(piece, piece, device(*flip))

    from_x, from_y, from_xy = {}, {}, {}
    from_sib = [[] for _ in range(teams)]
    own_hidden = [[] for _ in range(teams)]

    def start_own(i):
        from_x[i, 0] = send_own(X, i, 0)
        from_y[i, 1] = send_own(Y, i, 1)
        from_x[i, 1] = send_own(X, i, 1)
        from_y[i, 0] = send_own(Y, i, 0)
        for half in range(HALVES):
            from_sib[i].append(send_own(SIB, i, half))
            own_hidden[i].append(
                within(hid_ref.at[part(shards[i], half)], slots[i].at[place(mine, half)])
            )

    def sibling(panel, i, half):
        from_sib[i].append(forward(panel, SIB, i, half))

    def turn(i):
        from_x[i, 0].wait_recv()
        from_xy[i, 0] = forward(panel_x, Y, i, 0)
        from_y[i, 1].wait_recv()
        from_xy[i, 1] = forward(panel_y, X, i, 1)
        sibling(panel_x, i, 0)
        sibling(panel_y, i, 1)

    def rest(i):
        from_x[i, 1].wait_recv()
        sibling(panel_x, i, 1)
        from_y[i, 0].wait_recv()
        sibling(panel_y, i, 0)

    def corner(i):
        for half in range(HALVES):
            from_xy[i, half].wait_recv()
            sibling(panel_xy, i, half)

    def arrived(i):
        for copy in from_sib[i]:
            copy.wait_recv()
        for copy in own_hidden[i]:
            copy.wait()

    piece_rows = part_rows // PIECES
    per_half = PIECES // HALVES

    def landing(shard, panel, q):
        return gfull.at[
            shard, pl.ds((q // per_half) * panels + panel, 1), pl.ds(q % per_half * piece_rows, piece_rows)
        ]

    own_grad, own_pick, stage2 = [], [], []
    chain_base = send_sem.shape[0] - 2 * (teams - 1) * PIECES
    stage1_base = chain_base - (teams - 1) * PIECES

    def band(k, q):
        return pl.ds(k * part_rows + q * piece_rows, piece_rows)

    def spread(up, step, q, action):
        target = t + step if up else t - step

        @pl.when((target >= 0) & (target < teams))
        def _():
            at = stage1_base + (target + teams - t) % teams * PIECES - PIECES + q
            copy = remote(
                grad_ref.at[band(target, q)],
                gz.at[q, :, pl.ds(t * part_cols, part_cols)],
                (b, target, d),
                at,
            )
            action(copy)

    def spread_start(step, q):
        for up in (True, False):
            spread(up, step, q, lambda copy: copy.start())

    def fetch_tables():
        return [within(owner_ref, owner), within(act_ref, act)]

    def own_columns():
        lanes = lax.broadcasted_iota(jnp.int32, cols_row.shape, 1)
        row = jnp.full(cols_row.shape, column_blocks, jnp.int32)
        ranks = [jnp.int32(k * capacity) for k in range(owners_count)]
        for c in range(column_blocks):
            slot = ranks[0]
            holds = [owner[c] == k for k in range(owners_count)]
            for k in range(1, owners_count):
                slot = jnp.where(holds[k], ranks[k], slot)
            row = jnp.where(lanes == slot, c, row)
            ranks = [jnp.where(holds[k], ranks[k] + 1, ranks[k]) for k in range(owners_count)]
        cols_row[...] = row

    def own_rows():
        def column(j, carry):
            c = jnp.minimum(cols[0, mine * picks + j], column_blocks - 1)
            for k in range(per_column):
                rows_ref[j * per_column + k] = act[k, 0, c]
            return carry

        lax.fori_loop(0, picks, column, 0)

    def pick_columns(q):
        own_grad[q].wait()
        for step in range(1, teams):
            spread(True, step, q, lambda copy: copy.wait_recv())
            spread(False, step, q, lambda copy: copy.wait_recv())
        for c in range(column_blocks):
            gcol[q, c] = gz[q, :, c * BS : (c + 1) * BS]
        gcol[q, column_blocks] = jnp.zeros(gcol.shape[2:], gcol.dtype)

        def pick(p, carry):
            for j in range(picks):
                snd[q, p, :, j * BS : (j + 1) * BS] = gcol[q, cols[0, p * picks + j]]
            return carry

        lax.fori_loop(0, panels, pick, 0)
        for flip in flips:
            stage2.append(
                remote(snd.at[q, pl.ds(panel_of(*flip), 1)], landing(t, mine, q), device(*flip))
            )
        own_pick.append(within(snd.at[q, pl.ds(mine, 1)], landing(t, mine, q)))

    def picked(q):
        own_pick[q].wait()
        for copy in stage2[q * len(flips) : (q + 1) * len(flips)]:
            copy.wait_recv()

    def chain(up, k, shard, target, q):
        piece = gfull.at[
            shard, pl.ds((q // per_half) * panels, panels), pl.ds(q % per_half * piece_rows, piece_rows)
        ]
        step = k if up else teams - 1 + k
        return remote(piece, piece, (b, target, d), chain_base + step * PIECES + q)

    def chain_send(k, half, wait):
        @pl.when((t < teams - 1) & (t - k >= 0))
        def _():
            copy = chain(True, k, t - k, t + 1, half)
            copy.wait_send() if wait else copy.start()

        @pl.when((t > 0) & (t + k < teams))
        def _():
            copy = chain(False, k, t + k, t - 1, half)
            copy.wait_send() if wait else copy.start()

    def chain_step(k, half):
        @pl.when(t - 1 - k >= 0)
        def _():
            chain(True, k, t - 1 - k, t - 1, half).wait_recv()

        @pl.when(t + 1 + k < teams)
        def _():
            chain(False, k, t + 1 + k, t + 1, half).wait_recv()

        if k < teams - 2:
            chain_send(k + 1, half, False)

    def accumulate(i, lo, hi):
        def column(j, carry):
            g = gfull[shards[i], :, :, pl.ds(pl.multiple_of(j * BS, BS), BS)].reshape(-1, BS)
            for k in range(0, per_column, GROUP):
                first = j * per_column + k
                block = products(slots[i], rows_ref, first, GROUP, g)
                at = pl.ds(first, GROUP)
                acc[at] = block if i == 0 else acc[at] + block
            return carry

        lax.fori_loop(lo, hi, column, 0)

    middle = picks // 2
    start_own(0)
    for q in range(PIECES):
        own_grad.append(
            within(grad_ref.at[band(t, q)], gz.at[q, :, pl.ds(t * part_cols, part_cols)])
        )
    early = PIECES // 2
    for q in range(early):
        spread_start(1, q)
    tables = fetch_tables()
    for k in range(1, max(3, teams - 1)):
        met(ready.at[k - 1])
        if k < max(3, teams - 1) - 1:
            greet(ready.at[k])
        if k + 1 < teams:
            for q in range(early):
                spread_start(k + 1, q)
    for q in range(early, PIECES):
        for k in range(1, teams):
            spread_start(k, q)
    for copy in tables:
        copy.wait()
    own_columns()
    moved = within(cols_row, cols)
    moved.wait()
    pick_columns(0)
    pick_columns(1)
    turn(0)
    pick_columns(2)
    picked(0)
    chain_send(0, 0, False)
    pick_columns(3)
    start_own(1)
    picked(1)
    chain_send(0, 1, False)
    rest(0)
    picked(2)
    chain_send(0, 2, False)
    picked(3)
    chain_send(0, 3, False)
    own_rows()
    corner(0)
    arrived(0)
    accumulate(0, 0, middle)
    for i in range(1, teams):
        chain_step(i - 1, 0)
        turn(i)
        if i + 1 < teams:
            start_own(i + 1)
        chain_step(i - 1, 1)
        accumulate(i - 1, middle, picks)
        chain_step(i - 1, 2)
        rest(i)
        corner(i)
        chain_step(i - 1, 3)
        arrived(i)
        if i + 1 < teams:
            accumulate(i, 0, middle)
    for copy in sent:
        copy.wait_send()
    for q in range(PIECES):
        for k in range(1, teams):
            spread(True, k, q, lambda copy: copy.wait_send())
            spread(False, k, q, lambda copy: copy.wait_send())
        for k in range(teams - 1):
            chain_send(k, q, True)


def gather(col_owner, act_rows, hidden, out_grad, panels, picks):
    teams = lax.axis_size("team")
    panel_rows, units = hidden.shape
    per_column = act_rows.shape[0]
    part_rows = panel_rows // teams
    half_rows = part_rows // HALVES
    piece_rows = part_rows // PIECES
    group = panels * part_rows
    column_blocks = col_owner.shape[0]
    lanes = pl.cdiv(panels * picks, BS) * BS
    copies = (3 * (teams - 1) + panels - 1) * PIECES + 7 * HALVES * teams
    operands = (col_owner, act_rows, hidden, out_grad)
    hbm = pl.BlockSpec(memory_space=pltpu.HBM)
    smem = pl.BlockSpec(memory_space=pltpu.SMEM)
    vmem = pl.BlockSpec(memory_space=pltpu.VMEM)
    return pl.pallas_call(
        gather_kernel,
        out_shape=(
            pltpu.VMEM((group, units), hidden.dtype),
            pltpu.VMEM((teams, HALVES * panels, half_rows, picks * BS), out_grad.dtype),
            pltpu.VMEM((picks * per_column, BS, BS), jnp.float32),
            pltpu.SMEM((picks * per_column,), jnp.int32),
        ),
        in_specs=[hbm] * 4,
        out_specs=(vmem, vmem, vmem, smem),
        scratch_shapes=[pltpu.VMEM((group, units), hidden.dtype)] * (teams - 1)
        + [
            pltpu.VMEM((PIECES, piece_rows, column_blocks * BS), out_grad.dtype),
            pltpu.VMEM((PIECES, column_blocks + 1, piece_rows, BS), out_grad.dtype),
            pltpu.VMEM((PIECES, panels, piece_rows, picks * BS), out_grad.dtype),
            pltpu.SMEM(col_owner.shape, jnp.int32),
            pltpu.SMEM(act_rows.shape, jnp.int32),
            pltpu.VMEM((1, lanes), jnp.int32),
            pltpu.SMEM((1, lanes), jnp.int32),
            pltpu.SemaphoreType.REGULAR((max(3, teams - 1) - 1,)),
            pltpu.SemaphoreType.DMA((copies,)),
            pltpu.SemaphoreType.DMA((copies,)),
            pltpu.SemaphoreType.DMA((2 * PIECES + HALVES * teams + 3,)),
        ],
        compiler_params=pltpu.CompilerParams(
            collective_id=0, has_side_effects=True, vmem_limit_bytes=24 << 20
        ),
    )(*(pltpu.with_memory_space_constraint(x, pltpu.HBM) for x in operands))


def finish_kernel(rows_ref, h_ref, g_ref, acc_ref, out_ref, score_ref, buf, ssq, row, sem):
    teams = g_ref.shape[0]
    picks = g_ref.shape[-1] // BS
    slots = buf.shape[0]
    per_column = slots // picks
    shard = shard_of(teams - 1, lax.axis_index("team"), teams)
    ssq[slots:] = jnp.zeros((ssq.shape[0] - slots, BS), jnp.float32)
    copies = []
    for j in range(picks):
        g = g_ref[shard, :, :, j * BS : (j + 1) * BS].reshape(-1, BS)
        for first in range(j * per_column, (j + 1) * per_column, GROUP):
            at = slice(first, first + GROUP)
            block = acc_ref[at] + products(h_ref, rows_ref, first, GROUP, g)
            buf[at] = block
            ssq[at, :] = jnp.sum(block * block, axis=1)
        done = pl.ds(j * per_column, per_column)
        copies.append(pltpu.make_async_copy(buf.at[done], out_ref.at[done], sem.at[j]))
        copies[j].start()
    total = jnp.sum(ssq[...].T, axis=0, keepdims=True)
    scores = jnp.sqrt(total * (1.0 / (BS * BS)) + epsilon)
    row[...] = scores[:, :slots]
    copies.append(pltpu.make_async_copy(row, score_ref, sem.at[picks]))
    copies[picks].start()
    for copy in copies:
        copy.wait()


def finish(rows, last, grad, acc):
    slots = rows.shape[0]
    picks = grad.shape[-1] // BS
    hbm = pl.BlockSpec(memory_space=pltpu.HBM)
    smem = pl.BlockSpec(memory_space=pltpu.SMEM)
    vmem = pl.BlockSpec(memory_space=pltpu.VMEM)
    return pl.pallas_call(
        finish_kernel,
        out_shape=(
            jax.ShapeDtypeStruct((slots, BS, BS), jnp.float32),
            jax.ShapeDtypeStruct((1, slots), jnp.float32),
        ),
        in_specs=[smem, vmem, vmem, vmem],
        out_specs=(hbm, hbm),
        scratch_shapes=[
            pltpu.VMEM((slots, BS, BS), jnp.float32),
            pltpu.VMEM((pl.cdiv(slots, BS) * BS, BS), jnp.float32),
            pltpu.VMEM((1, slots), jnp.float32),
            pltpu.SemaphoreType.DMA((picks + 1,)),
        ],
        compiler_params=pltpu.CompilerParams(vmem_limit_bytes=20 << 20),
    )(rows, last, grad, acc)


def in_plane(hidden, out_grad, act_rows, col_owner):
    owners_count, cores = lax.axis_size("blk"), lax.axis_size("dp")
    column_blocks = col_owner.shape[0]
    capacity = min(3 * column_blocks // (2 * owners_count), 3 * column_blocks // 4)
    last, grad, acc, rows = gather(
        col_owner,
        jnp.transpose(act_rows, (2, 0, 1)),
        hidden,
        out_grad,
        owners_count * cores,
        capacity // cores,
    )
    gradients, scores = finish(rows, last, grad, acc)
    return (gradients[None, None], scores[None])


def on_device(hidden, out_grad, act_rows, col_owner):
    owners_count = lax.axis_size("blk")
    owner_index = lax.axis_index("blk")
    column_blocks = col_owner.shape[0]
    capacity = min(3 * column_blocks // (2 * owners_count), 3 * column_blocks // 4)
    per_column = act_rows.shape[2]
    owned_all, alive_all = owner_tables(col_owner, owners_count, capacity)
    owned_mine = lax.dynamic_index_in_dim(owned_all, owner_index, 0, keepdims=False)
    alive_mine = lax.dynamic_index_in_dim(alive_all, owner_index, 0, keepdims=False)
    block_rows = jnp.take(act_rows[0], owned_mine, axis=0).reshape(-1)
    grad_full = lax.all_gather(out_grad, "team", axis=1, tiled=True)
    grad_mask = alive_mine.astype(jnp.bfloat16)[None, :, None]
    hidden_piece = lax.all_gather(hidden, "blk", axis=0, tiled=True)
    grad_piece = lax.all_gather(grad_full, "blk", axis=0, tiled=True)
    count_rows = grad_piece.shape[0]
    picked_grad = (
        jnp.take(grad_piece.reshape(count_rows, column_blocks, BS), owned_mine, axis=1) * grad_mask
    )
    hidden_blocks = hidden_piece.reshape(count_rows, -1, BS)
    picked_hidden = jnp.take(hidden_blocks, block_rows, axis=1).reshape(
        count_rows, capacity, per_column, BS
    )
    partial_value = jnp.einsum(
        "ncki,ncj->ckij", picked_hidden, picked_grad, preferred_element_type=jnp.float32
    )
    partial_value = partial_value.reshape(capacity * per_column, BS, BS)
    gradients = lax.psum_scatter(partial_value, "dp", scatter_dimension=0, tiled=True)
    scores = jnp.sqrt(jnp.mean(gradients * gradients, axis=(1, 2)) + epsilon)
    return (gradients[None, None], scores[None, None])


def solution(mesh):
    in_specs = (P(("blk", "dp"), "team"), P(("blk", "dp"), "team"), P("team", None, None), P())
    out_specs = (P("team", "blk", "dp", None, None), P("team", "blk", "dp"))
    square = mesh.shape["blk"] == 4 and mesh.shape["dp"] == 2
    return jax.shard_map(
        in_plane if square else on_device,
        mesh=mesh,
        in_specs=in_specs,
        out_specs=out_specs,
        check_vma=False,
    )
```

```python
import jax
import jax.numpy as jnp
from jax import lax
from jax.experimental import pallas as pl
from jax.experimental.pallas import tpu as pltpu
from jax.sharding import PartitionSpec as P

BS = 128
MESH = pl.DeviceIdType.MESH
HALVES = 2
PIECES = 4
TAIL = 4
GROUP = 4


epsilon = 1e-06


def owner_tables(col_owner, owners_count, capacity):
    column_blocks = col_owner.shape[0]
    owners = jnp.arange(owners_count, dtype=jnp.int32)
    onehot = (col_owner[:, None] == owners[None, :]).astype(jnp.int32)
    column_rank = jnp.sum((jnp.cumsum(onehot, axis=0) - onehot) * onehot, axis=1)
    slot_ids = jnp.arange(capacity, dtype=jnp.int32)
    matches = (col_owner[None, None, :] == owners[:, None, None]) & (
        column_rank[None, None, :] == slot_ids[None, :, None]
    )
    owned_all = jnp.sum(
        matches.astype(jnp.int32) * jnp.arange(column_blocks, dtype=jnp.int32)[None, None, :],
        axis=2,
    )
    return owned_all, jnp.any(matches, axis=2)


def shard_of(i, t, teams):
    paired = 2 * jnp.minimum(t, teams - 1 - t)
    step = (i + 1) // 2
    near = t - step if i % 2 else t + step
    far = jnp.where(2 * t < teams, i, teams - 1 - i)
    return jnp.where(i <= paired, near, far)


def columns_of(slot, rows_ref, first, count):
    return [
        slot[:, pl.ds(rows_ref[first + i] * BS, BS)] for i in range(count)
    ]


def products(slot, rows_ref, first, count, g):
    return lax.dot_general(
        jnp.concatenate(columns_of(slot, rows_ref, first, count), axis=1),
        g,
        (((0,), (0,)), ((), ())),
        preferred_element_type=jnp.float32,
    ).reshape(count, BS, BS)


def gather_kernel(
    owner_ref, act_ref, hid_ref, grad_ref, last_ref, gfull, acc, rows_ref, *scratch
):
    *slots, gz, gcol, snd, owner, act, cols_row, cols, ready, send_sem, recv_sem, local_sem = scratch
    slots = [*slots, last_ref]
    teams = lax.axis_size("team")
    b, t, d = lax.axis_index("blk"), lax.axis_index("team"), lax.axis_index("dp")
    y, x = b // 2, b % 2
    _, panels, _, width = snd.shape
    picks = width // BS
    per_column = rows_ref.shape[0] // picks
    column_blocks = owner.shape[0]
    owners_count = lax.axis_size("blk")
    capacity = panels * picks // owners_count
    part_rows = hid_ref.shape[0] // teams
    half_rows = part_rows // HALVES
    part_cols = grad_ref.shape[1]

    def plane(sy, sx, sd):
        oy = 1 - y if sy else y
        ox = 1 - x if sx else x
        return oy * 2 + ox, (1 - d if sd else d)

    def panel_of(sy, sx, sd):
        ob, od = plane(sy, sx, sd)
        return ob * 2 + od

    def device(sy, sx, sd):
        ob, od = plane(sy, sx, sd)
        return (ob, t, od)

    mine = panel_of(0, 0, 0)
    flips = [(sy, sx, sd) for sy in (0, 1) for sx in (0, 1) for sd in (0, 1)][1:]

    barrier = pltpu.get_barrier_semaphore()
    X, Y, SIB = (0, 1, 0), (1, 0, 0), (0, 0, 1)
    below, above = (t > 0).astype(jnp.int32), (t < teams - 1).astype(jnp.int32)

    def greet(sem):
        for flip in (X, Y, SIB):
            pl.semaphore_signal(sem, inc=1, device_id=device(*flip), device_id_type=MESH)

        @pl.when(t > 0)
        def _():
            pl.semaphore_signal(sem, inc=1, device_id=(b, t - 1, d), device_id_type=MESH)

        @pl.when(t < teams - 1)
        def _():
            pl.semaphore_signal(sem, inc=1, device_id=(b, t + 1, d), device_id_type=MESH)

    def met(sem):
        pl.semaphore_wait(sem, 3 + below + above)

    greet(barrier)
    for step in range(2, teams):

        @pl.when(t + step < teams)
        def _():
            pl.semaphore_signal(
                barrier, inc=1, device_id=(b, t + step, d), device_id_type=MESH
            )

    pl.semaphore_wait(barrier, 3 + below + above + jnp.maximum(t - 1, 0))
    greet(ready.at[0])

    counter = [0, 0]
    sent, local = [], []

    def remote(src, dst, target, slot=None):
        started = slot is None
        if started:
            slot = counter[0]
            counter[0] += 1
        copy = pltpu.make_async_remote_copy(
            src_ref=src,
            dst_ref=dst,
            send_sem=send_sem.at[slot],
            recv_sem=recv_sem.at[slot],
            device_id=target,
            device_id_type=MESH,
        )
        if started:
            copy.start()
            sent.append(copy)
        return copy

    def within(src, dst):
        copy = pltpu.make_async_copy(src, dst, local_sem.at[counter[1]])
        counter[1] += 1
        copy.start()
        return copy

    from_me, by_x, by_y, by_xy = 0, 2, 4, 6

    def part(k, half):
        return pl.ds(k * part_rows + half * half_rows, half_rows)

    def place(rel, half):
        return pl.ds(rel * part_rows + half * half_rows, half_rows)

    shards = [shard_of(i, t, teams) for i in range(teams)]
    units = hid_ref.shape[1]

    def cuts(parts):
        return [pl.ds(k * (units // parts), units // parts) for k in range(parts)]

    def send_own(flip, i, half, cut=slice(None)):
        rel = flip[0] * 4 + flip[1] * 2 + flip[2]
        return remote(
            hid_ref.at[part(shards[i], half), cut],
            slots[i].at[place(rel, half), cut],
            device(*flip),
        )

    def forward(rel, flip, i, half, cut=slice(None)):
        there = rel ^ (flip[0] * 4 + flip[1] * 2 + flip[2])
        return remote(
            slots[i].at[place(rel, half), cut],
            slots[i].at[place(there, half), cut],
            device(*flip),
        )

    from_x, from_y, from_xy = {}, {}, {}
    from_sib = [[] for _ in range(teams)]
    own_hidden = [[] for _ in range(teams)]

    def start_own(i, cut=None):
        if cut in (None, 0):
            from_x[i, 0] = [send_own(X, i, 0)]
            from_y[i, 1] = [send_own(Y, i, 1)]
            from_x[i, 1], from_y[i, 0] = [], []
        pieces = [slice(None)] if cut is None else [cuts(2)[cut]]
        for piece in pieces:
            from_x[i, 1].append(send_own(X, i, 1, piece))
            from_y[i, 0].append(send_own(Y, i, 0, piece))
        if cut == 0:
            return
        for half in range(HALVES):
            from_sib[i].append(send_own(SIB, i, half))
            own_hidden[i].append(
                within(hid_ref.at[part(shards[i], half)], slots[i].at[place(from_me, half)])
            )

    def received(copies):
        for copy in copies:
            copy.wait_recv()

    def sibling(rel, i, half, cut=slice(None)):
        from_sib[i].append(forward(rel, SIB, i, half, cut))

    both = []

    def bands(i):
        if i < teams - 1:
            return [slice(None)]
        return [pl.ds(0, units - units // TAIL), pl.ds(units - units // TAIL, units // TAIL)]

    def turn(i):
        received(from_x[i, 0])
        from_xy[i, 0] = [forward(by_x, Y, i, 0, cut) for cut in bands(i)]
        received(from_y[i, 1])
        from_xy[i, 1] = [forward(by_y, X, i, 1, cut) for cut in bands(i)]
        if i == teams - 1:
            both.append(forward(by_x, (1, 0, 1), i, 0, bands(i)[1]))
            both.append(forward(by_y, (0, 1, 1), i, 1, bands(i)[1]))
        sibling(by_x, i, 0)
        sibling(by_y, i, 1)

    def rest(i):
        received(from_x[i, 1])
        sibling(by_x, i, 1)
        received(from_y[i, 0])
        sibling(by_y, i, 0)

    def corner(i):
        for half in range(HALVES):
            received(from_xy[i, half][:1])
            sibling(by_xy, i, half, bands(i)[0])
        for half in range(HALVES):
            received(from_xy[i, half][1:])
        if i == teams - 1:
            received(both)

    def arrived(i):
        for copy in from_sib[i]:
            copy.wait_recv()
        for copy in own_hidden[i]:
            copy.wait()

    piece_rows = part_rows // PIECES

    def landing(shard, rel, q):
        return gfull.at[shard, pl.ds(rel, 1), pl.ds(q * piece_rows, piece_rows)]

    own_grad, own_pick, stage2 = [], [], []
    chain_base = send_sem.shape[0] - 2 * (teams - 1) * PIECES
    stage1_base = chain_base - (teams - 1) * PIECES

    def band(k, q):
        return pl.ds(k * part_rows + q * piece_rows, piece_rows)

    def spread(up, step, q, action):
        target = t + step if up else t - step

        @pl.when((target >= 0) & (target < teams))
        def _():
            at = stage1_base + (target + teams - t) % teams * PIECES - PIECES + q
            copy = remote(
                grad_ref.at[band(target, q)],
                gz.at[q, :, pl.ds(t * part_cols, part_cols)],
                (b, target, d),
                at,
            )
            action(copy)

    def spread_start(up, step, q):
        spread(up, step, q, lambda copy: copy.start())

    def fetch_tables():
        return [within(owner_ref, owner), within(act_ref, act)]

    def own_columns():
        lanes = lax.broadcasted_iota(jnp.int32, cols_row.shape, 1)
        row = jnp.full(cols_row.shape, column_blocks, jnp.int32)
        ranks = [jnp.int32(k * capacity) for k in range(owners_count)]
        for c in range(column_blocks):
            slot = ranks[0]
            holds = [owner[c] == k for k in range(owners_count)]
            for k in range(1, owners_count):
                slot = jnp.where(holds[k], ranks[k], slot)
            row = jnp.where(lanes == slot, c, row)
            ranks = [jnp.where(holds[k], ranks[k] + 1, ranks[k]) for k in range(owners_count)]
        cols_row[...] = row

    def own_rows():
        def column(j, carry):
            c = jnp.minimum(cols[0, mine * picks + j], column_blocks - 1)
            for k in range(per_column):
                rows_ref[j * per_column + k] = act[k, 0, c]
            return carry

        lax.fori_loop(0, picks, column, 0)

    def pick_columns(q):
        own_grad[q].wait()
        for step in range(1, teams):
            spread(True, step, q, lambda copy: copy.wait_recv())
            spread(False, step, q, lambda copy: copy.wait_recv())
        for c in range(column_blocks):
            gcol[q, c] = gz[q, :, c * BS : (c + 1) * BS]
        gcol[q, column_blocks] = jnp.zeros(gcol.shape[2:], gcol.dtype)

        def pick(p, carry):
            for j in range(picks):
                snd[q, p, :, j * BS : (j + 1) * BS] = gcol[q, cols[0, p * picks + j]]
            return carry

        lax.fori_loop(0, panels, pick, 0)
        for flip in flips:
            stage2.append(
                remote(
                    snd.at[q, pl.ds(panel_of(*flip), 1)],
                    landing(t, flip[0] * 4 + flip[1] * 2 + flip[2], q),
                    device(*flip),
                )
            )
        own_pick.append(within(snd.at[q, pl.ds(mine, 1)], landing(t, from_me, q)))

    def picked(q):
        own_pick[q].wait()
        for copy in stage2[q * len(flips) : (q + 1) * len(flips)]:
            copy.wait_recv()

    def chain(up, k, shard, target, q):
        piece = gfull.at[shard, pl.ds(0, panels), pl.ds(q * piece_rows, piece_rows)]
        step = k if up else teams - 1 + k
        return remote(piece, piece, (b, target, d), chain_base + step * PIECES + q)

    def chain_send(k, half, wait):
        @pl.when((t < teams - 1) & (t - k >= 0))
        def _():
            copy = chain(True, k, t - k, t + 1, half)
            copy.wait_send() if wait else copy.start()

        @pl.when((t > 0) & (t + k < teams))
        def _():
            copy = chain(False, k, t + k, t - 1, half)
            copy.wait_send() if wait else copy.start()

    def chain_step(k, half):
        @pl.when(t - 1 - k >= 0)
        def _():
            chain(True, k, t - 1 - k, t - 1, half).wait_recv()

        @pl.when(t + 1 + k < teams)
        def _():
            chain(False, k, t + 1 + k, t + 1, half).wait_recv()

        if k < teams - 2:
            chain_send(k + 1, half, False)

    def accumulate(i, lo, hi):
        def column(j, carry):
            g = gfull[shards[i], :, :, pl.ds(pl.multiple_of(j * BS, BS), BS)].reshape(-1, BS)
            for k in range(0, per_column, GROUP):
                first = j * per_column + k
                block = products(slots[i], rows_ref, first, GROUP, g)
                at = pl.ds(first, GROUP)
                acc[at] = block if i == 0 else acc[at] + block
            return carry

        lax.fori_loop(lo, hi, column, 0)

    middle = picks // 2
    start_own(0, 0)
    for q in range(PIECES):
        own_grad.append(
            within(grad_ref.at[band(t, q)], gz.at[q, :, pl.ds(t * part_cols, part_cols)])
        )
    early = PIECES // 2
    for q in range(early):
        for k in range(teams - 1, 0, -1):
            spread_start(False, k, q)
        spread_start(True, 1, q)
    tables = fetch_tables()
    for k in range(1, max(3, teams - 1)):
        met(ready.at[k - 1])
        if k < max(3, teams - 1) - 1:
            greet(ready.at[k])
        if k + 1 < teams:
            for q in range(early):
                spread_start(True, k + 1, q)
    for q in range(early, PIECES):
        for k in range(teams - 1, 0, -1):
            spread_start(False, k, q)
            spread_start(True, k, q)
    for copy in tables:
        copy.wait()
    own_columns()
    moved = within(cols_row, cols)
    moved.wait()
    pick_columns(0)
    start_own(0, 1)
    pick_columns(1)
    pick_columns(2)
    picked(0)
    chain_send(0, 0, False)
    pick_columns(3)
    turn(0)
    start_own(1)
    picked(1)
    chain_send(0, 1, False)
    picked(2)
    chain_send(0, 2, False)
    rest(0)
    picked(3)
    chain_send(0, 3, False)
    own_rows()
    corner(0)
    arrived(0)
    accumulate(0, 0, middle)
    for i in range(1, teams):
        chain_step(i - 1, 0)
        turn(i)
        if i + 1 < teams:
            start_own(i + 1)
        chain_step(i - 1, 1)
        accumulate(i - 1, middle, picks)
        chain_step(i - 1, 2)
        rest(i)
        corner(i)
        chain_step(i - 1, 3)
        arrived(i)
        if i + 1 < teams:
            accumulate(i, 0, middle)
    for copy in sent:
        copy.wait_send()
    for q in range(PIECES):
        for k in range(1, teams):
            spread(True, k, q, lambda copy: copy.wait_send())
            spread(False, k, q, lambda copy: copy.wait_send())
        for k in range(teams - 1):
            chain_send(k, q, True)


def gather(col_owner, act_rows, hidden, out_grad, panels, picks):
    teams = lax.axis_size("team")
    panel_rows, units = hidden.shape
    per_column = act_rows.shape[0]
    part_rows = panel_rows // teams
    piece_rows = part_rows // PIECES
    group = panels * part_rows
    column_blocks = col_owner.shape[0]
    lanes = pl.cdiv(panels * picks, BS) * BS
    copies = (3 * (teams - 1) + panels - 1) * PIECES + 7 * HALVES * teams + 6
    operands = (col_owner, act_rows, hidden, out_grad)
    hbm = pl.BlockSpec(memory_space=pltpu.HBM)
    smem = pl.BlockSpec(memory_space=pltpu.SMEM)
    vmem = pl.BlockSpec(memory_space=pltpu.VMEM)
    return pl.pallas_call(
        gather_kernel,
        out_shape=(
            pltpu.VMEM((group, units), hidden.dtype),
            pltpu.VMEM((teams, panels, part_rows, picks * BS), out_grad.dtype),
            pltpu.VMEM((picks * per_column, BS, BS), jnp.float32),
            pltpu.SMEM((picks * per_column,), jnp.int32),
        ),
        in_specs=[hbm] * 4,
        out_specs=(vmem, vmem, vmem, smem),
        scratch_shapes=[pltpu.VMEM((group, units), hidden.dtype)] * (teams - 1)
        + [
            pltpu.VMEM((PIECES, piece_rows, column_blocks * BS), out_grad.dtype),
            pltpu.VMEM((PIECES, column_blocks + 1, piece_rows, BS), out_grad.dtype),
            pltpu.VMEM((PIECES, panels, piece_rows, picks * BS), out_grad.dtype),
            pltpu.SMEM(col_owner.shape, jnp.int32),
            pltpu.SMEM(act_rows.shape, jnp.int32),
            pltpu.VMEM((1, lanes), jnp.int32),
            pltpu.SMEM((1, lanes), jnp.int32),
            pltpu.SemaphoreType.REGULAR((max(3, teams - 1) - 1,)),
            pltpu.SemaphoreType.DMA((copies,)),
            pltpu.SemaphoreType.DMA((copies,)),
            pltpu.SemaphoreType.DMA((2 * PIECES + HALVES * teams + 3,)),
        ],
        compiler_params=pltpu.CompilerParams(
            collective_id=0, has_side_effects=True, vmem_limit_bytes=24 << 20
        ),
    )(*(pltpu.with_memory_space_constraint(x, pltpu.HBM) for x in operands))


def finish_kernel(rows_ref, h_ref, g_ref, acc_ref, out_ref, score_ref, buf, ssq, row, sem):
    teams = g_ref.shape[0]
    picks = g_ref.shape[-1] // BS
    slots = buf.shape[0]
    per_column = slots // picks
    shard = shard_of(teams - 1, lax.axis_index("team"), teams)
    ssq[slots:] = jnp.zeros((ssq.shape[0] - slots, BS), jnp.float32)
    copies = []
    for j in range(picks):
        g = g_ref[shard, :, :, j * BS : (j + 1) * BS].reshape(-1, BS)
        for first in range(j * per_column, (j + 1) * per_column, GROUP):
            at = slice(first, first + GROUP)
            block = acc_ref[at] + products(h_ref, rows_ref, first, GROUP, g)
            buf[at] = block
            ssq[at, :] = jnp.sum(block * block, axis=1)
        done = pl.ds(j * per_column, per_column)
        copies.append(pltpu.make_async_copy(buf.at[done], out_ref.at[done], sem.at[j]))
        copies[j].start()
    total = jnp.sum(ssq[...].T, axis=0, keepdims=True)
    scores = jnp.sqrt(total * (1.0 / (BS * BS)) + epsilon)
    row[...] = scores[:, :slots]
    copies.append(pltpu.make_async_copy(row, score_ref, sem.at[picks]))
    copies[picks].start()
    for copy in copies:
        copy.wait()


def finish(rows, last, grad, acc):
    slots = rows.shape[0]
    picks = grad.shape[-1] // BS
    hbm = pl.BlockSpec(memory_space=pltpu.HBM)
    smem = pl.BlockSpec(memory_space=pltpu.SMEM)
    vmem = pl.BlockSpec(memory_space=pltpu.VMEM)
    return pl.pallas_call(
        finish_kernel,
        out_shape=(
            jax.ShapeDtypeStruct((slots, BS, BS), jnp.float32),
            jax.ShapeDtypeStruct((1, slots), jnp.float32),
        ),
        in_specs=[smem, vmem, vmem, vmem],
        out_specs=(hbm, hbm),
        scratch_shapes=[
            pltpu.VMEM((slots, BS, BS), jnp.float32),
            pltpu.VMEM((pl.cdiv(slots, BS) * BS, BS), jnp.float32),
            pltpu.VMEM((1, slots), jnp.float32),
            pltpu.SemaphoreType.DMA((picks + 1,)),
        ],
        compiler_params=pltpu.CompilerParams(vmem_limit_bytes=20 << 20),
    )(rows, last, grad, acc)


def in_plane(hidden, out_grad, act_rows, col_owner):
    owners_count, cores = lax.axis_size("blk"), lax.axis_size("dp")
    column_blocks = col_owner.shape[0]
    capacity = min(3 * column_blocks // (2 * owners_count), 3 * column_blocks // 4)
    last, grad, acc, rows = gather(
        col_owner,
        jnp.transpose(act_rows, (2, 0, 1)),
        hidden,
        out_grad,
        owners_count * cores,
        capacity // cores,
    )
    gradients, scores = finish(rows, last, grad, acc)
    return (gradients[None, None], scores[None])


def on_device(hidden, out_grad, act_rows, col_owner):
    owners_count = lax.axis_size("blk")
    owner_index = lax.axis_index("blk")
    column_blocks = col_owner.shape[0]
    capacity = min(3 * column_blocks // (2 * owners_count), 3 * column_blocks // 4)
    per_column = act_rows.shape[2]
    owned_all, alive_all = owner_tables(col_owner, owners_count, capacity)
    owned_mine = lax.dynamic_index_in_dim(owned_all, owner_index, 0, keepdims=False)
    alive_mine = lax.dynamic_index_in_dim(alive_all, owner_index, 0, keepdims=False)
    block_rows = jnp.take(act_rows[0], owned_mine, axis=0).reshape(-1)
    grad_full = lax.all_gather(out_grad, "team", axis=1, tiled=True)
    grad_mask = alive_mine.astype(jnp.bfloat16)[None, :, None]
    hidden_piece = lax.all_gather(hidden, "blk", axis=0, tiled=True)
    grad_piece = lax.all_gather(grad_full, "blk", axis=0, tiled=True)
    count_rows = grad_piece.shape[0]
    picked_grad = (
        jnp.take(grad_piece.reshape(count_rows, column_blocks, BS), owned_mine, axis=1) * grad_mask
    )
    hidden_blocks = hidden_piece.reshape(count_rows, -1, BS)
    picked_hidden = jnp.take(hidden_blocks, block_rows, axis=1).reshape(
        count_rows, capacity, per_column, BS
    )
    partial_value = jnp.einsum(
        "ncki,ncj->ckij", picked_hidden, picked_grad, preferred_element_type=jnp.float32
    )
    partial_value = partial_value.reshape(capacity * per_column, BS, BS)
    gradients = lax.psum_scatter(partial_value, "dp", scatter_dimension=0, tiled=True)
    scores = jnp.sqrt(jnp.mean(gradients * gradients, axis=(1, 2)) + epsilon)
    return (gradients[None, None], scores[None, None])


def solution(mesh):
    in_specs = (P(("blk", "dp"), "team"), P(("blk", "dp"), "team"), P("team", None, None), P())
    out_specs = (P("team", "blk", "dp", None, None), P("team", "blk", "dp"))
    square = mesh.shape["blk"] == 4 and mesh.shape["dp"] == 2
    return jax.shard_map(
        in_plane if square else on_device,
        mesh=mesh,
        in_specs=in_specs,
        out_specs=out_specs,
        check_vma=False,
    )
```

```python
import jax
import jax.numpy as jnp
from jax import lax
from jax.experimental import pallas as pl
from jax.experimental.pallas import tpu as pltpu
from jax.sharding import PartitionSpec as P

BS = 128
MESH = pl.DeviceIdType.MESH
HALVES = 2
PIECES = 4
TAIL = 4
GROUP = 4
LAST = 3


epsilon = 1e-06


def owner_tables(col_owner, owners_count, capacity):
    column_blocks = col_owner.shape[0]
    owners = jnp.arange(owners_count, dtype=jnp.int32)
    onehot = (col_owner[:, None] == owners[None, :]).astype(jnp.int32)
    column_rank = jnp.sum((jnp.cumsum(onehot, axis=0) - onehot) * onehot, axis=1)
    slot_ids = jnp.arange(capacity, dtype=jnp.int32)
    matches = (col_owner[None, None, :] == owners[:, None, None]) & (
        column_rank[None, None, :] == slot_ids[None, :, None]
    )
    owned_all = jnp.sum(
        matches.astype(jnp.int32) * jnp.arange(column_blocks, dtype=jnp.int32)[None, None, :],
        axis=2,
    )
    return owned_all, jnp.any(matches, axis=2)


def shard_of(i, t, teams):
    paired = 2 * jnp.minimum(t, teams - 1 - t)
    step = (i + 1) // 2
    near = t - step if i % 2 else t + step
    far = jnp.where(2 * t < teams, i, teams - 1 - i)
    return jnp.where(i <= paired, near, far)


def columns_of(slot, rows_ref, first, count):
    return [
        slot[:, pl.ds(rows_ref[first + i] * BS, BS)] for i in range(count)
    ]


def products(slot, rows_ref, first, count, g):
    return lax.dot_general(
        jnp.concatenate(columns_of(slot, rows_ref, first, count), axis=1),
        g,
        (((0,), (0,)), ((), ())),
        preferred_element_type=jnp.float32,
    ).reshape(count, BS, BS)


def gather_kernel(
    owner_ref, act_ref, hid_ref, grad_ref, last_ref, gfull, acc, rows_ref, *scratch
):
    *slots, gz, gcol, snd, owner, act, cols_row, cols, ready, send_sem, recv_sem, local_sem = scratch
    slots = [*slots, last_ref]
    teams = lax.axis_size("team")
    b, t, d = lax.axis_index("blk"), lax.axis_index("team"), lax.axis_index("dp")
    y, x = b // 2, b % 2
    _, panels, _, width = snd.shape
    picks = width // BS
    per_column = rows_ref.shape[0] // picks
    column_blocks = owner.shape[0]
    owners_count = lax.axis_size("blk")
    capacity = panels * picks // owners_count
    part_rows = hid_ref.shape[0] // teams
    half_rows = part_rows // HALVES
    part_cols = grad_ref.shape[1]

    def plane(sy, sx, sd):
        oy = 1 - y if sy else y
        ox = 1 - x if sx else x
        return oy * 2 + ox, (1 - d if sd else d)

    def panel_of(sy, sx, sd):
        ob, od = plane(sy, sx, sd)
        return ob * 2 + od

    def device(sy, sx, sd):
        ob, od = plane(sy, sx, sd)
        return (ob, t, od)

    mine = panel_of(0, 0, 0)
    flips = [(sy, sx, sd) for sy in (0, 1) for sx in (0, 1) for sd in (0, 1)][1:]

    barrier = pltpu.get_barrier_semaphore()
    X, Y, SIB = (0, 1, 0), (1, 0, 0), (0, 0, 1)
    below, above = (t > 0).astype(jnp.int32), (t < teams - 1).astype(jnp.int32)

    def greet(sem):
        for flip in (X, Y, SIB):
            pl.semaphore_signal(sem, inc=1, device_id=device(*flip), device_id_type=MESH)

        @pl.when(t > 0)
        def _():
            pl.semaphore_signal(sem, inc=1, device_id=(b, t - 1, d), device_id_type=MESH)

        @pl.when(t < teams - 1)
        def _():
            pl.semaphore_signal(sem, inc=1, device_id=(b, t + 1, d), device_id_type=MESH)

    def met(sem):
        pl.semaphore_wait(sem, 3 + below + above)

    greet(barrier)
    for step in range(2, teams):

        @pl.when(t + step < teams)
        def _():
            pl.semaphore_signal(
                barrier, inc=1, device_id=(b, t + step, d), device_id_type=MESH
            )

    pl.semaphore_wait(barrier, 3 + below + above + jnp.maximum(t - 1, 0))
    greet(ready.at[0])

    counter = [0, 0]
    sent, local = [], []

    def remote(src, dst, target, slot=None):
        started = slot is None
        if started:
            slot = counter[0]
            counter[0] += 1
        copy = pltpu.make_async_remote_copy(
            src_ref=src,
            dst_ref=dst,
            send_sem=send_sem.at[slot],
            recv_sem=recv_sem.at[slot],
            device_id=target,
            device_id_type=MESH,
        )
        if started:
            copy.start()
            sent.append(copy)
        return copy

    def within(src, dst):
        copy = pltpu.make_async_copy(src, dst, local_sem.at[counter[1]])
        counter[1] += 1
        copy.start()
        return copy

    from_me, by_x, by_y, by_xy = 0, 2, 4, 6

    def part(k, half):
        return pl.ds(k * part_rows + half * half_rows, half_rows)

    def place(rel, half):
        return pl.ds(rel * part_rows + half * half_rows, half_rows)

    shards = [shard_of(i, t, teams) for i in range(teams)]
    units = hid_ref.shape[1]

    def cuts(parts):
        return [pl.ds(k * (units // parts), units // parts) for k in range(parts)]

    def send_own(flip, i, half, cut=slice(None)):
        rel = flip[0] * 4 + flip[1] * 2 + flip[2]
        return remote(
            hid_ref.at[part(shards[i], half), cut],
            slots[i].at[place(rel, half), cut],
            device(*flip),
        )

    def forward(rel, flip, i, half, cut=slice(None)):
        there = rel ^ (flip[0] * 4 + flip[1] * 2 + flip[2])
        return remote(
            slots[i].at[place(rel, half), cut],
            slots[i].at[place(there, half), cut],
            device(*flip),
        )

    from_x, from_y, from_xy = {}, {}, {}
    from_sib = [[] for _ in range(teams)]
    own_hidden = [[] for _ in range(teams)]

    def start_own(i, cut=None):
        if cut in (None, 0):
            from_x[i, 0] = [send_own(X, i, 0)]
            from_y[i, 1] = [send_own(Y, i, 1)]
            from_x[i, 1], from_y[i, 0] = [], []
        pieces = [slice(None)] if cut is None else [cuts(2)[cut]]
        for piece in pieces:
            from_x[i, 1].append(send_own(X, i, 1, piece))
            from_y[i, 0].append(send_own(Y, i, 0, piece))
        if cut == 0:
            return
        for half in range(HALVES):
            from_sib[i].append(send_own(SIB, i, half))
            own_hidden[i].append(
                within(hid_ref.at[part(shards[i], half)], slots[i].at[place(from_me, half)])
            )

    def received(copies):
        for copy in copies:
            copy.wait_recv()

    def sibling(rel, i, half, cut=slice(None)):
        from_sib[i].append(forward(rel, SIB, i, half, cut))

    both = []

    def bands(i):
        if i < teams - 1:
            return [slice(None)]
        return [pl.ds(0, units - units // TAIL), pl.ds(units - units // TAIL, units // TAIL)]

    def turn(i):
        received(from_x[i, 0])
        from_xy[i, 0] = [forward(by_x, Y, i, 0, cut) for cut in bands(i)]
        received(from_y[i, 1])
        from_xy[i, 1] = [forward(by_y, X, i, 1, cut) for cut in bands(i)]
        if i == teams - 1:
            both.append(forward(by_x, (1, 0, 1), i, 0, bands(i)[1]))
            both.append(forward(by_y, (0, 1, 1), i, 1, bands(i)[1]))
        sibling(by_x, i, 0)
        sibling(by_y, i, 1)

    def rest(i):
        received(from_x[i, 1])
        sibling(by_x, i, 1)
        received(from_y[i, 0])
        sibling(by_y, i, 0)

    def corner(i):
        for half in range(HALVES):
            received(from_xy[i, half][:1])
            sibling(by_xy, i, half, bands(i)[0])
        for half in range(HALVES):
            received(from_xy[i, half][1:])
        if i == teams - 1:
            received(both)

    def arrived(i):
        for copy in from_sib[i]:
            copy.wait_recv()
        for copy in own_hidden[i]:
            copy.wait()

    piece_rows = part_rows // PIECES

    def landing(shard, rel, q):
        return gfull.at[shard, pl.ds(rel, 1), pl.ds(q * piece_rows, piece_rows)]

    own_grad, own_pick, stage2 = [], [], []
    chain_base = send_sem.shape[0] - 2 * (teams - 1) * PIECES
    stage1_base = chain_base - (teams - 1) * PIECES

    def band(k, q):
        return pl.ds(k * part_rows + q * piece_rows, piece_rows)

    def spread(up, step, q, action):
        target = t + step if up else t - step

        @pl.when((target >= 0) & (target < teams))
        def _():
            at = stage1_base + (target + teams - t) % teams * PIECES - PIECES + q
            copy = remote(
                grad_ref.at[band(target, q)],
                gz.at[q, :, pl.ds(t * part_cols, part_cols)],
                (b, target, d),
                at,
            )
            action(copy)

    def spread_start(up, step, q):
        spread(up, step, q, lambda copy: copy.start())

    def fetch_tables():
        return [within(owner_ref, owner), within(act_ref, act)]

    def own_columns():
        lanes = lax.broadcasted_iota(jnp.int32, cols_row.shape, 1)
        row = jnp.full(cols_row.shape, column_blocks, jnp.int32)
        ranks = [jnp.int32(k * capacity) for k in range(owners_count)]
        for c in range(column_blocks):
            slot = ranks[0]
            holds = [owner[c] == k for k in range(owners_count)]
            for k in range(1, owners_count):
                slot = jnp.where(holds[k], ranks[k], slot)
            row = jnp.where(lanes == slot, c, row)
            ranks = [jnp.where(holds[k], ranks[k] + 1, ranks[k]) for k in range(owners_count)]
        cols_row[...] = row

    def own_rows():
        def column(j, carry):
            c = jnp.minimum(cols[0, mine * picks + j], column_blocks - 1)
            for k in range(per_column):
                rows_ref[j * per_column + k] = act[k, 0, c]
            return carry

        lax.fori_loop(0, picks, column, 0)

    def pick_columns(q):
        own_grad[q].wait()
        for step in range(1, teams):
            spread(True, step, q, lambda copy: copy.wait_recv())
            spread(False, step, q, lambda copy: copy.wait_recv())
        for c in range(column_blocks):
            gcol[q, c] = gz[q, :, c * BS : (c + 1) * BS]
        gcol[q, column_blocks] = jnp.zeros(gcol.shape[2:], gcol.dtype)

        def pick(p, carry):
            for j in range(picks):
                snd[q, p, :, j * BS : (j + 1) * BS] = gcol[q, cols[0, p * picks + j]]
            return carry

        lax.fori_loop(0, panels, pick, 0)
        for flip in flips:
            stage2.append(
                remote(
                    snd.at[q, pl.ds(panel_of(*flip), 1)],
                    landing(t, flip[0] * 4 + flip[1] * 2 + flip[2], q),
                    device(*flip),
                )
            )
        own_pick.append(within(snd.at[q, pl.ds(mine, 1)], landing(t, from_me, q)))

    def picked(q):
        own_pick[q].wait()
        for copy in stage2[q * len(flips) : (q + 1) * len(flips)]:
            copy.wait_recv()

    def chain(up, k, shard, target, q):
        piece = gfull.at[shard, pl.ds(0, panels), pl.ds(q * piece_rows, piece_rows)]
        step = k if up else teams - 1 + k
        return remote(piece, piece, (b, target, d), chain_base + step * PIECES + q)

    def chain_send(k, half, wait):
        @pl.when((t < teams - 1) & (t - k >= 0))
        def _():
            copy = chain(True, k, t - k, t + 1, half)
            copy.wait_send() if wait else copy.start()

        @pl.when((t > 0) & (t + k < teams))
        def _():
            copy = chain(False, k, t + k, t - 1, half)
            copy.wait_send() if wait else copy.start()

    def chain_step(k, half):
        @pl.when(t - 1 - k >= 0)
        def _():
            chain(True, k, t - 1 - k, t - 1, half).wait_recv()

        @pl.when(t + 1 + k < teams)
        def _():
            chain(False, k, t + 1 + k, t + 1, half).wait_recv()

        if k < teams - 2:
            chain_send(k + 1, half, False)

    def accumulate(i, lo, hi):
        def column(j, carry):
            g = gfull[shards[i], :, :, pl.ds(pl.multiple_of(j * BS, BS), BS)].reshape(-1, BS)
            for k in range(0, per_column, GROUP):
                first = j * per_column + k
                block = products(slots[i], rows_ref, first, GROUP, g)
                at = pl.ds(first, GROUP)
                acc[at] = block if i == 0 else acc[at] + block
            return carry

        lax.fori_loop(lo, hi, column, 0)

    def settle():
        for copy in sent[:early]:
            copy.wait_send()
        for q in range(PIECES):
            for k in range(1, teams):
                spread(True, k, q, lambda copy: copy.wait_send())
                spread(False, k, q, lambda copy: copy.wait_send())
            for k in range(teams - 2):
                chain_send(k, q, True)

    middle = picks // 2
    start_own(0, 0)
    for q in range(PIECES):
        own_grad.append(
            within(grad_ref.at[band(t, q)], gz.at[q, :, pl.ds(t * part_cols, part_cols)])
        )
    first = PIECES // 2
    for q in range(first):
        for k in range(teams - 1, 0, -1):
            spread_start(False, k, q)
        spread_start(True, 1, q)
    tables = fetch_tables()
    for k in range(1, max(3, teams - 1)):
        met(ready.at[k - 1])
        if k < max(3, teams - 1) - 1:
            greet(ready.at[k])
        if k + 1 < teams:
            for q in range(first):
                spread_start(True, k + 1, q)
    for q in range(first, PIECES):
        for k in range(teams - 1, 0, -1):
            spread_start(False, k, q)
            spread_start(True, k, q)
    for copy in tables:
        copy.wait()
    own_columns()
    moved = within(cols_row, cols)
    moved.wait()
    pick_columns(0)
    start_own(0, 1)
    pick_columns(1)
    pick_columns(2)
    picked(0)
    chain_send(0, 0, False)
    pick_columns(3)
    turn(0)
    start_own(1)
    picked(1)
    chain_send(0, 1, False)
    picked(2)
    chain_send(0, 2, False)
    rest(0)
    picked(3)
    chain_send(0, 3, False)
    own_rows()
    corner(0)
    arrived(0)
    accumulate(0, 0, middle)
    for i in range(1, teams):
        chain_step(i - 1, 0)
        early = len(sent)
        turn(i)
        if i + 1 < teams:
            start_own(i + 1)
        chain_step(i - 1, 1)
        accumulate(i - 1, middle, picks)
        chain_step(i - 1, 2)
        rest(i)
        if i + 1 == teams:
            settle()
        corner(i)
        chain_step(i - 1, 3)
        arrived(i)
        if i + 1 < teams:
            accumulate(i, 0, middle)
    for copy in sent[early:]:
        copy.wait_send()
    for q in range(PIECES):
        chain_send(teams - 2, q, True)


def gather(col_owner, act_rows, hidden, out_grad, panels, picks):
    teams = lax.axis_size("team")
    panel_rows, units = hidden.shape
    per_column = act_rows.shape[0]
    part_rows = panel_rows // teams
    piece_rows = part_rows // PIECES
    group = panels * part_rows
    column_blocks = col_owner.shape[0]
    lanes = pl.cdiv(panels * picks, BS) * BS
    copies = (3 * (teams - 1) + panels - 1) * PIECES + 7 * HALVES * teams + 6
    operands = (col_owner, act_rows, hidden, out_grad)
    hbm = pl.BlockSpec(memory_space=pltpu.HBM)
    smem = pl.BlockSpec(memory_space=pltpu.SMEM)
    vmem = pl.BlockSpec(memory_space=pltpu.VMEM)
    return pl.pallas_call(
        gather_kernel,
        out_shape=(
            pltpu.VMEM((group, units), hidden.dtype),
            pltpu.VMEM((teams, panels, part_rows, picks * BS), out_grad.dtype),
            pltpu.VMEM((picks * per_column, BS, BS), jnp.float32),
            pltpu.SMEM((picks * per_column,), jnp.int32),
        ),
        in_specs=[hbm] * 4,
        out_specs=(vmem, vmem, vmem, smem),
        scratch_shapes=[pltpu.VMEM((group, units), hidden.dtype)] * (teams - 1)
        + [
            pltpu.VMEM((PIECES, piece_rows, column_blocks * BS), out_grad.dtype),
            pltpu.VMEM((PIECES, column_blocks + 1, piece_rows, BS), out_grad.dtype),
            pltpu.VMEM((PIECES, panels, piece_rows, picks * BS), out_grad.dtype),
            pltpu.SMEM(col_owner.shape, jnp.int32),
            pltpu.SMEM(act_rows.shape, jnp.int32),
            pltpu.VMEM((1, lanes), jnp.int32),
            pltpu.SMEM((1, lanes), jnp.int32),
            pltpu.SemaphoreType.REGULAR((max(3, teams - 1) - 1,)),
            pltpu.SemaphoreType.DMA((copies,)),
            pltpu.SemaphoreType.DMA((copies,)),
            pltpu.SemaphoreType.DMA((2 * PIECES + HALVES * teams + 3,)),
        ],
        compiler_params=pltpu.CompilerParams(
            collective_id=0, has_side_effects=True, vmem_limit_bytes=24 << 20
        ),
    )(*(pltpu.with_memory_space_constraint(x, pltpu.HBM) for x in operands))


def finish_kernel(rows_ref, h_ref, g_ref, acc_ref, out_ref, score_ref, buf, ssq, row, sem):
    teams = g_ref.shape[0]
    picks = g_ref.shape[-1] // BS
    slots = buf.shape[0]
    per_column = slots // picks
    shard = shard_of(teams - 1, lax.axis_index("team"), teams)
    ssq[slots:] = jnp.zeros((ssq.shape[0] - slots, BS), jnp.float32)
    copies = []
    for j in range(picks):
        g = g_ref[shard, :, :, j * BS : (j + 1) * BS].reshape(-1, BS)
        for first in range(j * per_column, (j + 1) * per_column, LAST):
            at = slice(first, first + LAST)
            block = acc_ref[at] + products(h_ref, rows_ref, first, LAST, g)
            buf[at] = block
            ssq[at, :] = jnp.sum(block * block, axis=1)
        done = pl.ds(j * per_column, per_column)
        copies.append(pltpu.make_async_copy(buf.at[done], out_ref.at[done], sem.at[j]))
        copies[j].start()
    total = jnp.sum(ssq[...].T, axis=0, keepdims=True)
    scores = jnp.sqrt(total * (1.0 / (BS * BS)) + epsilon)
    row[...] = scores[:, :slots]
    copies.append(pltpu.make_async_copy(row, score_ref, sem.at[picks]))
    copies[picks].start()
    for copy in copies:
        copy.wait()


def finish(rows, last, grad, acc):
    slots = rows.shape[0]
    picks = grad.shape[-1] // BS
    hbm = pl.BlockSpec(memory_space=pltpu.HBM)
    smem = pl.BlockSpec(memory_space=pltpu.SMEM)
    vmem = pl.BlockSpec(memory_space=pltpu.VMEM)
    return pl.pallas_call(
        finish_kernel,
        out_shape=(
            jax.ShapeDtypeStruct((slots, BS, BS), jnp.float32),
            jax.ShapeDtypeStruct((1, slots), jnp.float32),
        ),
        in_specs=[smem, vmem, vmem, vmem],
        out_specs=(hbm, hbm),
        scratch_shapes=[
            pltpu.VMEM((slots, BS, BS), jnp.float32),
            pltpu.VMEM((pl.cdiv(slots, BS) * BS, BS), jnp.float32),
            pltpu.VMEM((1, slots), jnp.float32),
            pltpu.SemaphoreType.DMA((picks + 1,)),
        ],
        compiler_params=pltpu.CompilerParams(vmem_limit_bytes=20 << 20),
    )(rows, last, grad, acc)


def in_plane(hidden, out_grad, act_rows, col_owner):
    owners_count, cores = lax.axis_size("blk"), lax.axis_size("dp")
    column_blocks = col_owner.shape[0]
    capacity = min(3 * column_blocks // (2 * owners_count), 3 * column_blocks // 4)
    last, grad, acc, rows = gather(
        col_owner,
        jnp.transpose(act_rows, (2, 0, 1)),
        hidden,
        out_grad,
        owners_count * cores,
        capacity // cores,
    )
    gradients, scores = finish(rows, last, grad, acc)
    return (gradients[None, None], scores[None])


def on_device(hidden, out_grad, act_rows, col_owner):
    owners_count = lax.axis_size("blk")
    owner_index = lax.axis_index("blk")
    column_blocks = col_owner.shape[0]
    capacity = min(3 * column_blocks // (2 * owners_count), 3 * column_blocks // 4)
    per_column = act_rows.shape[2]
    owned_all, alive_all = owner_tables(col_owner, owners_count, capacity)
    owned_mine = lax.dynamic_index_in_dim(owned_all, owner_index, 0, keepdims=False)
    alive_mine = lax.dynamic_index_in_dim(alive_all, owner_index, 0, keepdims=False)
    block_rows = jnp.take(act_rows[0], owned_mine, axis=0).reshape(-1)
    grad_full = lax.all_gather(out_grad, "team", axis=1, tiled=True)
    grad_mask = alive_mine.astype(jnp.bfloat16)[None, :, None]
    hidden_piece = lax.all_gather(hidden, "blk", axis=0, tiled=True)
    grad_piece = lax.all_gather(grad_full, "blk", axis=0, tiled=True)
    count_rows = grad_piece.shape[0]
    picked_grad = (
        jnp.take(grad_piece.reshape(count_rows, column_blocks, BS), owned_mine, axis=1) * grad_mask
    )
    hidden_blocks = hidden_piece.reshape(count_rows, -1, BS)
    picked_hidden = jnp.take(hidden_blocks, block_rows, axis=1).reshape(
        count_rows, capacity, per_column, BS
    )
    partial_value = jnp.einsum(
        "ncki,ncj->ckij", picked_hidden, picked_grad, preferred_element_type=jnp.float32
    )
    partial_value = partial_value.reshape(capacity * per_column, BS, BS)
    gradients = lax.psum_scatter(partial_value, "dp", scatter_dimension=0, tiled=True)
    scores = jnp.sqrt(jnp.mean(gradients * gradients, axis=(1, 2)) + epsilon)
    return (gradients[None, None], scores[None, None])


def solution(mesh):
    in_specs = (P(("blk", "dp"), "team"), P(("blk", "dp"), "team"), P("team", None, None), P())
    out_specs = (P("team", "blk", "dp", None, None), P("team", "blk", "dp"))
    square = mesh.shape["blk"] == 4 and mesh.shape["dp"] == 2
    return jax.shard_map(
        in_plane if square else on_device,
        mesh=mesh,
        in_specs=in_specs,
        out_specs=out_specs,
        check_vma=False,
    )
```

```python
import jax
import jax.numpy as jnp
from jax import lax
from jax.experimental import pallas as pl
from jax.experimental.pallas import tpu as pltpu
from jax.sharding import PartitionSpec as P

BS = 128
MESH = pl.DeviceIdType.MESH
HALVES = 2
PIECES = 4
TAIL = 4
GROUP = 4
LAST = 3


epsilon = 1e-06


def owner_tables(col_owner, owners_count, capacity):
    column_blocks = col_owner.shape[0]
    owners = jnp.arange(owners_count, dtype=jnp.int32)
    onehot = (col_owner[:, None] == owners[None, :]).astype(jnp.int32)
    column_rank = jnp.sum((jnp.cumsum(onehot, axis=0) - onehot) * onehot, axis=1)
    slot_ids = jnp.arange(capacity, dtype=jnp.int32)
    matches = (col_owner[None, None, :] == owners[:, None, None]) & (
        column_rank[None, None, :] == slot_ids[None, :, None]
    )
    owned_all = jnp.sum(
        matches.astype(jnp.int32) * jnp.arange(column_blocks, dtype=jnp.int32)[None, None, :],
        axis=2,
    )
    return owned_all, jnp.any(matches, axis=2)


def shard_of(i, t, teams):
    paired = 2 * jnp.minimum(t, teams - 1 - t)
    step = (i + 1) // 2
    near = t - step if i % 2 else t + step
    far = jnp.where(2 * t < teams, i, teams - 1 - i)
    return jnp.where(i <= paired, near, far)


def columns_of(slot, rows_ref, first, count):
    return [
        slot[:, pl.ds(rows_ref[first + i] * BS, BS)] for i in range(count)
    ]


def products(slot, rows_ref, first, count, g):
    return lax.dot_general(
        jnp.concatenate(columns_of(slot, rows_ref, first, count), axis=1),
        g,
        (((0,), (0,)), ((), ())),
        preferred_element_type=jnp.float32,
    ).reshape(count, BS, BS)


def gather_kernel(
    owner_ref, act_ref, hid_ref, grad_ref, last_ref, gfull, acc, rows_ref, *scratch
):
    *slots, gz, gcol, snd, owner, act, cols_row, cols, ready, send_sem, recv_sem, local_sem = scratch
    slots = [*slots, last_ref]
    teams = lax.axis_size("team")
    b, t, d = lax.axis_index("blk"), lax.axis_index("team"), lax.axis_index("dp")
    y, x = b // 2, b % 2
    _, panels, _, width = snd.shape
    picks = width // BS
    per_column = rows_ref.shape[0] // picks
    column_blocks = owner.shape[0]
    owners_count = lax.axis_size("blk")
    capacity = panels * picks // owners_count
    part_rows = hid_ref.shape[0] // teams
    half_rows = part_rows // HALVES
    part_cols = grad_ref.shape[1]

    def plane(sy, sx, sd):
        oy = 1 - y if sy else y
        ox = 1 - x if sx else x
        return oy * 2 + ox, (1 - d if sd else d)

    def panel_of(sy, sx, sd):
        ob, od = plane(sy, sx, sd)
        return ob * 2 + od

    def device(sy, sx, sd):
        ob, od = plane(sy, sx, sd)
        return (ob, t, od)

    mine = panel_of(0, 0, 0)
    flips = [(sy, sx, sd) for sy in (0, 1) for sx in (0, 1) for sd in (0, 1)][1:]

    barrier = pltpu.get_barrier_semaphore()
    X, Y, SIB = (0, 1, 0), (1, 0, 0), (0, 0, 1)
    below, above = (t > 0).astype(jnp.int32), (t < teams - 1).astype(jnp.int32)

    def greet(sem):
        for flip in (X, Y, SIB):
            pl.semaphore_signal(sem, inc=1, device_id=device(*flip), device_id_type=MESH)

        @pl.when(t > 0)
        def _():
            pl.semaphore_signal(sem, inc=1, device_id=(b, t - 1, d), device_id_type=MESH)

        @pl.when(t < teams - 1)
        def _():
            pl.semaphore_signal(sem, inc=1, device_id=(b, t + 1, d), device_id_type=MESH)

    def met(sem):
        pl.semaphore_wait(sem, 3 + below + above)

    greet(barrier)
    for step in range(2, teams):

        @pl.when(t + step < teams)
        def _():
            pl.semaphore_signal(
                barrier, inc=1, device_id=(b, t + step, d), device_id_type=MESH
            )

    pl.semaphore_wait(barrier, 3 + below + above + jnp.maximum(t - 1, 0))
    greet(ready.at[0])

    counter = [0, 0]
    sent, local = [], []

    def remote(src, dst, target, slot=None):
        started = slot is None
        if started:
            slot = counter[0]
            counter[0] += 1
        copy = pltpu.make_async_remote_copy(
            src_ref=src,
            dst_ref=dst,
            send_sem=send_sem.at[slot],
            recv_sem=recv_sem.at[slot],
            device_id=target,
            device_id_type=MESH,
        )
        if started:
            copy.start()
            sent.append(copy)
        return copy

    def within(src, dst):
        copy = pltpu.make_async_copy(src, dst, local_sem.at[counter[1]])
        counter[1] += 1
        copy.start()
        return copy

    from_me, by_x, by_y, by_xy = 0, 2, 4, 6

    def part(k, half):
        return pl.ds(k * part_rows + half * half_rows, half_rows)

    def place(rel, half):
        return pl.ds(rel * part_rows + half * half_rows, half_rows)

    shards = [shard_of(i, t, teams) for i in range(teams)]
    units = hid_ref.shape[1]

    def cuts(parts):
        return [pl.ds(k * (units // parts), units // parts) for k in range(parts)]

    def send_own(flip, i, half, cut=slice(None)):
        rel = flip[0] * 4 + flip[1] * 2 + flip[2]
        return remote(
            hid_ref.at[part(shards[i], half), cut],
            slots[i].at[place(rel, half), cut],
            device(*flip),
        )

    def forward(rel, flip, i, half, cut=slice(None)):
        there = rel ^ (flip[0] * 4 + flip[1] * 2 + flip[2])
        return remote(
            slots[i].at[place(rel, half), cut],
            slots[i].at[place(there, half), cut],
            device(*flip),
        )

    from_x, from_y, from_xy = {}, {}, {}
    from_sib = [[] for _ in range(teams)]
    own_hidden = [[] for _ in range(teams)]

    def start_own(i, cut=None):
        if cut in (None, 0):
            from_x[i, 0] = [send_own(X, i, 0)]
            from_y[i, 1] = [send_own(Y, i, 1)]
            from_x[i, 1], from_y[i, 0] = [], []
        pieces = [slice(None)] if cut is None else [cuts(2)[cut]]
        for piece in pieces:
            from_x[i, 1].append(send_own(X, i, 1, piece))
            from_y[i, 0].append(send_own(Y, i, 0, piece))
        if cut == 0:
            return
        for half in range(HALVES):
            from_sib[i].append(send_own(SIB, i, half))
            own_hidden[i].append(
                within(hid_ref.at[part(shards[i], half)], slots[i].at[place(from_me, half)])
            )

    def received(copies):
        for copy in copies:
            copy.wait_recv()

    def sibling(rel, i, half, cut=slice(None)):
        from_sib[i].append(forward(rel, SIB, i, half, cut))

    both = []

    def bands(i):
        if i < teams - 1:
            return [slice(None)]
        return [pl.ds(0, units - units // TAIL), pl.ds(units - units // TAIL, units // TAIL)]

    def turn(i):
        received(from_x[i, 0])
        from_xy[i, 0] = [forward(by_x, Y, i, 0, cut) for cut in bands(i)]
        received(from_y[i, 1])
        from_xy[i, 1] = [forward(by_y, X, i, 1, cut) for cut in bands(i)]
        if i == teams - 1:
            both.append(forward(by_x, (1, 0, 1), i, 0, bands(i)[1]))
            both.append(forward(by_y, (0, 1, 1), i, 1, bands(i)[1]))
        sibling(by_x, i, 0)
        sibling(by_y, i, 1)

    def rest(i):
        received(from_x[i, 1])
        sibling(by_x, i, 1)
        received(from_y[i, 0])
        sibling(by_y, i, 0)

    def corner(i):
        for half in range(HALVES):
            received(from_xy[i, half][:1])
            sibling(by_xy, i, half, bands(i)[0])
        for half in range(HALVES):
            received(from_xy[i, half][1:])
        if i == teams - 1:
            received(both)

    def arrived(i):
        for copy in from_sib[i]:
            copy.wait_recv()
        for copy in own_hidden[i]:
            copy.wait()

    piece_rows = part_rows // PIECES

    def landing(shard, rel, q):
        return gfull.at[shard, pl.ds(rel, 1), pl.ds(q * piece_rows, piece_rows)]

    own_grad, own_pick, stage2 = [], [], []
    chain_base = send_sem.shape[0] - 2 * (teams - 1) * PIECES
    stage1_base = chain_base - (teams - 1) * PIECES

    def band(k, q):
        return pl.ds(k * part_rows + q * piece_rows, piece_rows)

    def spread(up, step, q, action):
        target = t + step if up else t - step

        @pl.when((target >= 0) & (target < teams))
        def _():
            at = stage1_base + (target + teams - t) % teams * PIECES - PIECES + q
            copy = remote(
                grad_ref.at[band(target, q)],
                gz.at[q, :, pl.ds(t * part_cols, part_cols)],
                (b, target, d),
                at,
            )
            action(copy)

    def spread_start(up, step, q):
        spread(up, step, q, lambda copy: copy.start())

    def fetch_tables():
        return [within(owner_ref, owner), within(act_ref, act)]

    def own_columns():
        lanes = lax.broadcasted_iota(jnp.int32, cols_row.shape, 1)
        row = jnp.full(cols_row.shape, column_blocks, jnp.int32)
        ranks = [jnp.int32(k * capacity) for k in range(owners_count)]
        for c in range(column_blocks):
            slot = ranks[0]
            holds = [owner[c] == k for k in range(owners_count)]
            for k in range(1, owners_count):
                slot = jnp.where(holds[k], ranks[k], slot)
            row = jnp.where(lanes == slot, c, row)
            ranks = [jnp.where(holds[k], ranks[k] + 1, ranks[k]) for k in range(owners_count)]
        cols_row[...] = row

    def own_rows():
        def column(j, carry):
            c = jnp.minimum(cols[0, mine * picks + j], column_blocks - 1)
            for k in range(per_column):
                rows_ref[j * per_column + k] = act[k, 0, c]
            return carry

        lax.fori_loop(0, picks, column, 0)

    def pick_columns(q):
        own_grad[q].wait()
        for step in range(1, teams):
            spread(True, step, q, lambda copy: copy.wait_recv())
            spread(False, step, q, lambda copy: copy.wait_recv())
        for c in range(column_blocks):
            gcol[q, c] = gz[q, :, c * BS : (c + 1) * BS]

        def pick(p, carry):
            for j in range(picks):
                snd[q, p, :, j * BS : (j + 1) * BS] = gcol[q, cols[0, p * picks + j]]
            return carry

        lax.fori_loop(0, panels, pick, 0)
        for flip in flips:
            stage2.append(
                remote(
                    snd.at[q, pl.ds(panel_of(*flip), 1)],
                    landing(t, flip[0] * 4 + flip[1] * 2 + flip[2], q),
                    device(*flip),
                )
            )
        own_pick.append(within(snd.at[q, pl.ds(mine, 1)], landing(t, from_me, q)))

    def picked(q):
        own_pick[q].wait()
        for copy in stage2[q * len(flips) : (q + 1) * len(flips)]:
            copy.wait_recv()

    def chain(up, k, shard, target, q):
        piece = gfull.at[shard, pl.ds(0, panels), pl.ds(q * piece_rows, piece_rows)]
        step = k if up else teams - 1 + k
        return remote(piece, piece, (b, target, d), chain_base + step * PIECES + q)

    def chain_send(k, half, wait):
        @pl.when((t < teams - 1) & (t - k >= 0))
        def _():
            copy = chain(True, k, t - k, t + 1, half)
            copy.wait_send() if wait else copy.start()

        @pl.when((t > 0) & (t + k < teams))
        def _():
            copy = chain(False, k, t + k, t - 1, half)
            copy.wait_send() if wait else copy.start()

    def chain_step(k, half):
        @pl.when(t - 1 - k >= 0)
        def _():
            chain(True, k, t - 1 - k, t - 1, half).wait_recv()

        @pl.when(t + 1 + k < teams)
        def _():
            chain(False, k, t + 1 + k, t + 1, half).wait_recv()

        if k < teams - 2:
            chain_send(k + 1, half, False)

    def accumulate(i, lo, hi):
        def column(j, carry):
            g = gfull[shards[i], :, :, pl.ds(pl.multiple_of(j * BS, BS), BS)].reshape(-1, BS)
            for k in range(0, per_column, GROUP):
                first = j * per_column + k
                block = products(slots[i], rows_ref, first, GROUP, g)
                at = pl.ds(first, GROUP)
                acc[at] = block if i == 0 else acc[at] + block
            return carry

        lax.fori_loop(lo, hi, column, 0)

    def settle():
        for copy in sent[:early]:
            copy.wait_send()
        for q in range(PIECES):
            for k in range(1, teams):
                spread(True, k, q, lambda copy: copy.wait_send())
                spread(False, k, q, lambda copy: copy.wait_send())
            for k in range(teams - 2):
                chain_send(k, q, True)

    middle = picks // 2
    start_own(0, 0)
    for q in range(PIECES):
        own_grad.append(
            within(grad_ref.at[band(t, q)], gz.at[q, :, pl.ds(t * part_cols, part_cols)])
        )
    first = PIECES // 2
    for q in range(first):
        for k in range(teams - 1, 0, -1):
            spread_start(False, k, q)
        spread_start(True, 1, q)
    tables = fetch_tables()
    for k in range(1, max(3, teams - 1)):
        met(ready.at[k - 1])
        if k < max(3, teams - 1) - 1:
            greet(ready.at[k])
        if k + 1 < teams:
            for q in range(first):
                spread_start(True, k + 1, q)
    for q in range(first, PIECES):
        for k in range(teams - 1, 0, -1):
            spread_start(False, k, q)
            spread_start(True, k, q)
    for copy in tables:
        copy.wait()
    own_columns()
    for q in range(PIECES):
        gcol[q, column_blocks] = jnp.zeros(gcol.shape[2:], gcol.dtype)
    moved = within(cols_row, cols)
    moved.wait()
    pick_columns(0)
    start_own(0, 1)
    pick_columns(1)
    pick_columns(2)
    picked(0)
    chain_send(0, 0, False)
    pick_columns(3)
    turn(0)
    start_own(1)
    picked(1)
    chain_send(0, 1, False)
    picked(2)
    chain_send(0, 2, False)
    rest(0)
    picked(3)
    chain_send(0, 3, False)
    own_rows()
    corner(0)
    arrived(0)
    accumulate(0, 0, middle)
    for i in range(1, teams):
        chain_step(i - 1, 0)
        early = len(sent)
        turn(i)
        if i + 1 < teams:
            start_own(i + 1)
        chain_step(i - 1, 1)
        accumulate(i - 1, middle, picks)
        chain_step(i - 1, 2)
        rest(i)
        if i + 1 == teams:
            settle()
        corner(i)
        chain_step(i - 1, 3)
        arrived(i)
        if i + 1 < teams:
            accumulate(i, 0, middle)
    for copy in sent[early:]:
        copy.wait_send()
    for q in range(PIECES):
        chain_send(teams - 2, q, True)


def gather(col_owner, act_rows, hidden, out_grad, panels, picks):
    teams = lax.axis_size("team")
    panel_rows, units = hidden.shape
    per_column = act_rows.shape[0]
    part_rows = panel_rows // teams
    piece_rows = part_rows // PIECES
    group = panels * part_rows
    column_blocks = col_owner.shape[0]
    lanes = pl.cdiv(panels * picks, BS) * BS
    copies = (3 * (teams - 1) + panels - 1) * PIECES + 7 * HALVES * teams + 6
    operands = (col_owner, act_rows, hidden, out_grad)
    hbm = pl.BlockSpec(memory_space=pltpu.HBM)
    smem = pl.BlockSpec(memory_space=pltpu.SMEM)
    vmem = pl.BlockSpec(memory_space=pltpu.VMEM)
    return pl.pallas_call(
        gather_kernel,
        out_shape=(
            pltpu.VMEM((group, units), hidden.dtype),
            pltpu.VMEM((teams, panels, part_rows, picks * BS), out_grad.dtype),
            pltpu.VMEM((picks * per_column, BS, BS), jnp.float32),
            pltpu.SMEM((picks * per_column,), jnp.int32),
        ),
        in_specs=[hbm] * 4,
        out_specs=(vmem, vmem, vmem, smem),
        scratch_shapes=[pltpu.VMEM((group, units), hidden.dtype)] * (teams - 1)
        + [
            pltpu.VMEM((PIECES, piece_rows, column_blocks * BS), out_grad.dtype),
            pltpu.VMEM((PIECES, column_blocks + 1, piece_rows, BS), out_grad.dtype),
            pltpu.VMEM((PIECES, panels, piece_rows, picks * BS), out_grad.dtype),
            pltpu.SMEM(col_owner.shape, jnp.int32),
            pltpu.SMEM(act_rows.shape, jnp.int32),
            pltpu.VMEM((1, lanes), jnp.int32),
            pltpu.SMEM((1, lanes), jnp.int32),
            pltpu.SemaphoreType.REGULAR((max(3, teams - 1) - 1,)),
            pltpu.SemaphoreType.DMA((copies,)),
            pltpu.SemaphoreType.DMA((copies,)),
            pltpu.SemaphoreType.DMA((2 * PIECES + HALVES * teams + 3,)),
        ],
        compiler_params=pltpu.CompilerParams(
            collective_id=0, has_side_effects=True, vmem_limit_bytes=24 << 20
        ),
    )(*(pltpu.with_memory_space_constraint(x, pltpu.HBM) for x in operands))


def finish_kernel(rows_ref, h_ref, g_ref, acc_ref, out_ref, score_ref, buf, ssq, row, sem):
    teams = g_ref.shape[0]
    picks = g_ref.shape[-1] // BS
    slots = buf.shape[0]
    per_column = slots // picks
    shard = shard_of(teams - 1, lax.axis_index("team"), teams)
    ssq[slots:] = jnp.zeros((ssq.shape[0] - slots, BS), jnp.float32)
    copies = []
    for j in range(picks):
        g = g_ref[shard, :, :, j * BS : (j + 1) * BS].reshape(-1, BS)
        for first in range(j * per_column, (j + 1) * per_column, LAST):
            at = slice(first, first + LAST)
            block = acc_ref[at] + products(h_ref, rows_ref, first, LAST, g)
            buf[at] = block
            ssq[at, :] = jnp.sum(block * block, axis=1)
        done = pl.ds(j * per_column, per_column)
        copies.append(pltpu.make_async_copy(buf.at[done], out_ref.at[done], sem.at[j]))
        copies[j].start()
    total = jnp.sum(ssq[...].T, axis=0, keepdims=True)
    scores = jnp.sqrt(total * (1.0 / (BS * BS)) + epsilon)
    row[...] = scores[:, :slots]
    copies.append(pltpu.make_async_copy(row, score_ref, sem.at[picks]))
    copies[picks].start()
    for copy in copies:
        copy.wait()


def finish(rows, last, grad, acc):
    slots = rows.shape[0]
    picks = grad.shape[-1] // BS
    hbm = pl.BlockSpec(memory_space=pltpu.HBM)
    smem = pl.BlockSpec(memory_space=pltpu.SMEM)
    vmem = pl.BlockSpec(memory_space=pltpu.VMEM)
    return pl.pallas_call(
        finish_kernel,
        out_shape=(
            jax.ShapeDtypeStruct((slots, BS, BS), jnp.float32),
            jax.ShapeDtypeStruct((1, slots), jnp.float32),
        ),
        in_specs=[smem, vmem, vmem, vmem],
        out_specs=(hbm, hbm),
        scratch_shapes=[
            pltpu.VMEM((slots, BS, BS), jnp.float32),
            pltpu.VMEM((pl.cdiv(slots, BS) * BS, BS), jnp.float32),
            pltpu.VMEM((1, slots), jnp.float32),
            pltpu.SemaphoreType.DMA((picks + 1,)),
        ],
        compiler_params=pltpu.CompilerParams(vmem_limit_bytes=20 << 20),
    )(rows, last, grad, acc)


def in_plane(hidden, out_grad, act_rows, col_owner):
    owners_count, cores = lax.axis_size("blk"), lax.axis_size("dp")
    column_blocks = col_owner.shape[0]
    capacity = min(3 * column_blocks // (2 * owners_count), 3 * column_blocks // 4)
    last, grad, acc, rows = gather(
        col_owner,
        jnp.transpose(act_rows, (2, 0, 1)),
        hidden,
        out_grad,
        owners_count * cores,
        capacity // cores,
    )
    gradients, scores = finish(rows, last, grad, acc)
    return (gradients[None, None], scores[None])


def on_device(hidden, out_grad, act_rows, col_owner):
    owners_count = lax.axis_size("blk")
    owner_index = lax.axis_index("blk")
    column_blocks = col_owner.shape[0]
    capacity = min(3 * column_blocks // (2 * owners_count), 3 * column_blocks // 4)
    per_column = act_rows.shape[2]
    owned_all, alive_all = owner_tables(col_owner, owners_count, capacity)
    owned_mine = lax.dynamic_index_in_dim(owned_all, owner_index, 0, keepdims=False)
    alive_mine = lax.dynamic_index_in_dim(alive_all, owner_index, 0, keepdims=False)
    block_rows = jnp.take(act_rows[0], owned_mine, axis=0).reshape(-1)
    grad_full = lax.all_gather(out_grad, "team", axis=1, tiled=True)
    grad_mask = alive_mine.astype(jnp.bfloat16)[None, :, None]
    hidden_piece = lax.all_gather(hidden, "blk", axis=0, tiled=True)
    grad_piece = lax.all_gather(grad_full, "blk", axis=0, tiled=True)
    count_rows = grad_piece.shape[0]
    picked_grad = (
        jnp.take(grad_piece.reshape(count_rows, column_blocks, BS), owned_mine, axis=1) * grad_mask
    )
    hidden_blocks = hidden_piece.reshape(count_rows, -1, BS)
    picked_hidden = jnp.take(hidden_blocks, block_rows, axis=1).reshape(
        count_rows, capacity, per_column, BS
    )
    partial_value = jnp.einsum(
        "ncki,ncj->ckij", picked_hidden, picked_grad, preferred_element_type=jnp.float32
    )
    partial_value = partial_value.reshape(capacity * per_column, BS, BS)
    gradients = lax.psum_scatter(partial_value, "dp", scatter_dimension=0, tiled=True)
    scores = jnp.sqrt(jnp.mean(gradients * gradients, axis=(1, 2)) + epsilon)
    return (gradients[None, None], scores[None, None])


def solution(mesh):
    in_specs = (P(("blk", "dp"), "team"), P(("blk", "dp"), "team"), P("team", None, None), P())
    out_specs = (P("team", "blk", "dp", None, None), P("team", "blk", "dp"))
    square = mesh.shape["blk"] == 4 and mesh.shape["dp"] == 2
    return jax.shard_map(
        in_plane if square else on_device,
        mesh=mesh,
        in_specs=in_specs,
        out_specs=out_specs,
        check_vma=False,
    )
```

```python
import jax
import jax.numpy as jnp
from jax import lax
from jax.experimental import pallas as pl
from jax.experimental.pallas import tpu as pltpu
from jax.sharding import PartitionSpec as P

BS = 128
MESH = pl.DeviceIdType.MESH
HALVES = 2
PIECES = 4
TAIL = 4
GROUP = 4
LAST = 3


epsilon = 1e-06


def owner_tables(col_owner, owners_count, capacity):
    column_blocks = col_owner.shape[0]
    owners = jnp.arange(owners_count, dtype=jnp.int32)
    onehot = (col_owner[:, None] == owners[None, :]).astype(jnp.int32)
    column_rank = jnp.sum((jnp.cumsum(onehot, axis=0) - onehot) * onehot, axis=1)
    slot_ids = jnp.arange(capacity, dtype=jnp.int32)
    matches = (col_owner[None, None, :] == owners[:, None, None]) & (
        column_rank[None, None, :] == slot_ids[None, :, None]
    )
    owned_all = jnp.sum(
        matches.astype(jnp.int32) * jnp.arange(column_blocks, dtype=jnp.int32)[None, None, :],
        axis=2,
    )
    return owned_all, jnp.any(matches, axis=2)


def shard_of(i, t, teams):
    paired = 2 * jnp.minimum(t, teams - 1 - t)
    step = (i + 1) // 2
    near = t - step if i % 2 else t + step
    far = jnp.where(2 * t < teams, i, teams - 1 - i)
    return jnp.where(i <= paired, near, far)


def columns_of(slot, rows_ref, first, count):
    return [
        slot[:, pl.ds(rows_ref[first + i] * BS, BS)] for i in range(count)
    ]


def products(slot, rows_ref, first, count, g):
    return lax.dot_general(
        jnp.concatenate(columns_of(slot, rows_ref, first, count), axis=1),
        g,
        (((0,), (0,)), ((), ())),
        preferred_element_type=jnp.float32,
    ).reshape(count, BS, BS)


def gather_kernel(
    owner_ref, act_ref, hid_ref, grad_ref, last_ref, gfull, acc, rows_ref, *scratch
):
    *slots, gz, gcol, snd, owner, act, cols_row, cols, ready, send_sem, recv_sem, local_sem = scratch
    slots = [*slots, last_ref]
    teams = lax.axis_size("team")
    b, t, d = lax.axis_index("blk"), lax.axis_index("team"), lax.axis_index("dp")
    y, x = b // 2, b % 2
    _, panels, _, width = snd.shape
    picks = width // BS
    per_column = rows_ref.shape[0] // picks
    column_blocks = owner.shape[0]
    owners_count = lax.axis_size("blk")
    capacity = panels * picks // owners_count
    part_rows = hid_ref.shape[0] // teams
    half_rows = part_rows // HALVES
    part_cols = grad_ref.shape[1]

    def plane(sy, sx, sd):
        oy = 1 - y if sy else y
        ox = 1 - x if sx else x
        return oy * 2 + ox, (1 - d if sd else d)

    def panel_of(sy, sx, sd):
        ob, od = plane(sy, sx, sd)
        return ob * 2 + od

    def device(sy, sx, sd):
        ob, od = plane(sy, sx, sd)
        return (ob, t, od)

    mine = panel_of(0, 0, 0)
    flips = [(sy, sx, sd) for sy in (0, 1) for sx in (0, 1) for sd in (0, 1)][1:]

    barrier = pltpu.get_barrier_semaphore()
    X, Y, SIB = (0, 1, 0), (1, 0, 0), (0, 0, 1)
    below, above = (t > 0).astype(jnp.int32), (t < teams - 1).astype(jnp.int32)

    def greet(sem):
        for flip in (X, Y, SIB):
            pl.semaphore_signal(sem, inc=1, device_id=device(*flip), device_id_type=MESH)

        @pl.when(t > 0)
        def _():
            pl.semaphore_signal(sem, inc=1, device_id=(b, t - 1, d), device_id_type=MESH)

        @pl.when(t < teams - 1)
        def _():
            pl.semaphore_signal(sem, inc=1, device_id=(b, t + 1, d), device_id_type=MESH)

    def met(sem):
        pl.semaphore_wait(sem, 3 + below + above)

    greet(barrier)
    for step in range(2, teams):

        @pl.when(t + step < teams)
        def _():
            pl.semaphore_signal(
                barrier, inc=1, device_id=(b, t + step, d), device_id_type=MESH
            )

    pl.semaphore_wait(barrier, 3 + below + above + jnp.maximum(t - 1, 0))
    greet(ready.at[0])

    counter = [0, 0]
    sent, local = [], []

    def remote(src, dst, target, slot=None):
        started = slot is None
        if started:
            slot = counter[0]
            counter[0] += 1
        copy = pltpu.make_async_remote_copy(
            src_ref=src,
            dst_ref=dst,
            send_sem=send_sem.at[slot],
            recv_sem=recv_sem.at[slot],
            device_id=target,
            device_id_type=MESH,
        )
        if started:
            copy.start()
            sent.append(copy)
        return copy

    def within(src, dst):
        copy = pltpu.make_async_copy(src, dst, local_sem.at[counter[1]])
        counter[1] += 1
        copy.start()
        return copy

    from_me, by_x, by_y, by_xy = 0, 2, 4, 6

    def part(k, half):
        return pl.ds(k * part_rows + half * half_rows, half_rows)

    def place(rel, half):
        return pl.ds(rel * part_rows + half * half_rows, half_rows)

    shards = [shard_of(i, t, teams) for i in range(teams)]
    units = hid_ref.shape[1]

    def cuts(parts):
        return [pl.ds(k * (units // parts), units // parts) for k in range(parts)]

    def send_own(flip, i, half, cut=slice(None)):
        rel = flip[0] * 4 + flip[1] * 2 + flip[2]
        return remote(
            hid_ref.at[part(shards[i], half), cut],
            slots[i].at[place(rel, half), cut],
            device(*flip),
        )

    def forward(rel, flip, i, half, cut=slice(None)):
        there = rel ^ (flip[0] * 4 + flip[1] * 2 + flip[2])
        return remote(
            slots[i].at[place(rel, half), cut],
            slots[i].at[place(there, half), cut],
            device(*flip),
        )

    from_x, from_y, from_xy = {}, {}, {}
    from_sib = [[] for _ in range(teams)]
    own_hidden = [[] for _ in range(teams)]

    def start_own(i, cut=None):
        if cut in (None, 0):
            from_x[i, 0] = [send_own(X, i, 0)]
            from_y[i, 1] = [send_own(Y, i, 1)]
            from_x[i, 1], from_y[i, 0] = [], []
        pieces = [slice(None)] if cut is None else [cuts(2)[cut]]
        for piece in pieces:
            from_x[i, 1].append(send_own(X, i, 1, piece))
            from_y[i, 0].append(send_own(Y, i, 0, piece))
        if cut == 0:
            return
        for half in range(HALVES):
            from_sib[i].append(send_own(SIB, i, half))
            own_hidden[i].append(
                within(hid_ref.at[part(shards[i], half)], slots[i].at[place(from_me, half)])
            )

    def received(copies):
        for copy in copies:
            copy.wait_recv()

    def sibling(rel, i, half, cut=slice(None)):
        from_sib[i].append(forward(rel, SIB, i, half, cut))

    both = []

    def bands(i):
        if i < teams - 1:
            return [slice(None)]
        return [pl.ds(0, units - units // TAIL), pl.ds(units - units // TAIL, units // TAIL)]

    def turn(i):
        received(from_x[i, 0])
        from_xy[i, 0] = [forward(by_x, Y, i, 0, cut) for cut in bands(i)]
        received(from_y[i, 1])
        from_xy[i, 1] = [forward(by_y, X, i, 1, cut) for cut in bands(i)]
        if i == teams - 1:
            both.append(forward(by_x, (1, 0, 1), i, 0, bands(i)[1]))
            both.append(forward(by_y, (0, 1, 1), i, 1, bands(i)[1]))
        sibling(by_x, i, 0)
        sibling(by_y, i, 1)

    def rest(i):
        received(from_x[i, 1])
        sibling(by_x, i, 1)
        received(from_y[i, 0])
        sibling(by_y, i, 0)

    def corner(i):
        for half in range(HALVES):
            received(from_xy[i, half][:1])
            sibling(by_xy, i, half, bands(i)[0])
        for half in range(HALVES):
            received(from_xy[i, half][1:])
        if i == teams - 1:
            received(both)

    def arrived(i):
        for copy in from_sib[i]:
            copy.wait_recv()
        for copy in own_hidden[i]:
            copy.wait()

    piece_rows = part_rows // PIECES

    def landing(shard, rel, q):
        return gfull.at[shard, pl.ds(rel, 1), pl.ds(q * piece_rows, piece_rows)]

    own_grad, own_pick, stage2 = [], [], []
    chain_base = send_sem.shape[0] - 2 * (teams - 1) * PIECES
    stage1_base = chain_base - (teams - 1) * PIECES

    def band(k, q):
        return pl.ds(k * part_rows + q * piece_rows, piece_rows)

    def spread(up, step, q, action):
        target = t + step if up else t - step

        @pl.when((target >= 0) & (target < teams))
        def _():
            at = stage1_base + (target + teams - t) % teams * PIECES - PIECES + q
            copy = remote(
                grad_ref.at[band(target, q)],
                gz.at[q, :, pl.ds(t * part_cols, part_cols)],
                (b, target, d),
                at,
            )
            action(copy)

    def spread_start(up, step, q):
        spread(up, step, q, lambda copy: copy.start())

    def fetch_tables():
        return [within(owner_ref, owner), within(act_ref, act)]

    def own_columns():
        lanes = lax.broadcasted_iota(jnp.int32, cols_row.shape, 1)
        row = jnp.full(cols_row.shape, column_blocks, jnp.int32)
        ranks = [jnp.int32(k * capacity) for k in range(owners_count)]
        for c in range(column_blocks):
            slot = ranks[0]
            holds = [owner[c] == k for k in range(owners_count)]
            for k in range(1, owners_count):
                slot = jnp.where(holds[k], ranks[k], slot)
            row = jnp.where(lanes == slot, c, row)
            ranks = [jnp.where(holds[k], ranks[k] + 1, ranks[k]) for k in range(owners_count)]
        cols_row[...] = row

    def own_rows():
        def column(j, carry):
            c = jnp.minimum(cols[0, mine * picks + j], column_blocks - 1)
            for k in range(per_column):
                rows_ref[j * per_column + k] = act[k, 0, c]
            return carry

        lax.fori_loop(0, picks, column, 0)

    def pick_columns(q):
        own_grad[q].wait()
        for step in range(1, teams):
            spread(True, step, q, lambda copy: copy.wait_recv())
            spread(False, step, q, lambda copy: copy.wait_recv())
        for c in range(column_blocks):
            gcol[q, c] = gz[q, :, c * BS : (c + 1) * BS]

        def pick(p, carry):
            for j in range(picks):
                snd[q, p, :, j * BS : (j + 1) * BS] = gcol[q, cols[0, p * picks + j]]
            return carry

        lax.fori_loop(0, panels, pick, 0)
        for flip in flips:
            stage2.append(
                remote(
                    snd.at[q, pl.ds(panel_of(*flip), 1)],
                    landing(t, flip[0] * 4 + flip[1] * 2 + flip[2], q),
                    device(*flip),
                )
            )
        own_pick.append(within(snd.at[q, pl.ds(mine, 1)], landing(t, from_me, q)))

    def picked(q):
        own_pick[q].wait()
        for copy in stage2[q * len(flips) : (q + 1) * len(flips)]:
            copy.wait_recv()

    def chain(up, k, shard, target, q):
        piece = gfull.at[shard, pl.ds(0, panels), pl.ds(q * piece_rows, piece_rows)]
        step = k if up else teams - 1 + k
        return remote(piece, piece, (b, target, d), chain_base + step * PIECES + q)

    def chain_send(k, half, wait):
        @pl.when((t < teams - 1) & (t - k >= 0))
        def _():
            copy = chain(True, k, t - k, t + 1, half)
            copy.wait_send() if wait else copy.start()

        @pl.when((t > 0) & (t + k < teams))
        def _():
            copy = chain(False, k, t + k, t - 1, half)
            copy.wait_send() if wait else copy.start()

    def chain_step(k, half):
        @pl.when(t - 1 - k >= 0)
        def _():
            chain(True, k, t - 1 - k, t - 1, half).wait_recv()

        @pl.when(t + 1 + k < teams)
        def _():
            chain(False, k, t + 1 + k, t + 1, half).wait_recv()

        if k < teams - 2:
            chain_send(k + 1, half, False)

    def accumulate(i, lo, hi):
        def column(j, carry):
            g = gfull[shards[i], :, :, pl.ds(pl.multiple_of(j * BS, BS), BS)].reshape(-1, BS)
            for k in range(0, per_column, GROUP):
                first = j * per_column + k
                block = products(slots[i], rows_ref, first, GROUP, g)
                at = pl.ds(first, GROUP)
                acc[at] = block if i == 0 else acc[at] + block
            return carry

        lax.fori_loop(lo, hi, column, 0)

    def settle():
        for copy in sent[:early]:
            copy.wait_send()
        for q in range(PIECES):
            for k in range(1, teams):
                spread(True, k, q, lambda copy: copy.wait_send())
                spread(False, k, q, lambda copy: copy.wait_send())
            for k in range(teams - 2):
                chain_send(k, q, True)

    middle = picks // 2
    start_own(0, 0)
    for q in range(PIECES):
        own_grad.append(
            within(grad_ref.at[band(t, q)], gz.at[q, :, pl.ds(t * part_cols, part_cols)])
        )
    first = PIECES // 2
    for q in range(first):
        for k in range(teams - 1, 0, -1):
            spread_start(False, k, q)
        spread_start(True, 1, q)
    tables = fetch_tables()
    for k in range(1, max(3, teams - 1)):
        met(ready.at[k - 1])
        if k < max(3, teams - 1) - 1:
            greet(ready.at[k])
        if k + 1 < teams:
            for q in range(first):
                spread_start(True, k + 1, q)
    for q in range(first, PIECES):
        for k in range(teams - 1, 0, -1):
            spread_start(False, k, q)
            spread_start(True, k, q)
    for copy in tables:
        copy.wait()
    own_columns()
    for q in range(PIECES):
        gcol[q, column_blocks] = jnp.zeros(gcol.shape[2:], gcol.dtype)
    moved = within(cols_row, cols)
    moved.wait()
    pick_columns(0)
    start_own(0, 1)
    pick_columns(1)
    pick_columns(2)
    picked(0)
    chain_send(0, 0, False)
    pick_columns(3)
    turn(0)
    start_own(1)
    picked(1)
    chain_send(0, 1, False)
    picked(2)
    chain_send(0, 2, False)
    rest(0)
    picked(3)
    chain_send(0, 3, False)
    own_rows()
    corner(0)
    arrived(0)
    accumulate(0, 0, middle)
    for i in range(1, teams):
        chain_step(i - 1, 0)
        early = len(sent)
        turn(i)
        if i + 1 < teams:
            start_own(i + 1)
        chain_step(i - 1, 1)
        accumulate(i - 1, middle, picks)
        chain_step(i - 1, 2)
        rest(i)
        if i + 1 == teams:
            settle()
        corner(i)
        chain_step(i - 1, 3)
        arrived(i)
        if i + 1 < teams:
            accumulate(i, 0, middle)
    for copy in sent[early:]:
        copy.wait_send()
    for q in range(PIECES):
        chain_send(teams - 2, q, True)


def gather(col_owner, act_rows, hidden, out_grad, panels, picks):
    teams = lax.axis_size("team")
    panel_rows, units = hidden.shape
    per_column = act_rows.shape[0]
    part_rows = panel_rows // teams
    piece_rows = part_rows // PIECES
    group = panels * part_rows
    column_blocks = col_owner.shape[0]
    lanes = pl.cdiv(panels * picks, BS) * BS
    copies = (3 * (teams - 1) + panels - 1) * PIECES + 7 * HALVES * teams + 6
    operands = (col_owner, act_rows, hidden, out_grad)
    hbm = pl.BlockSpec(memory_space=pltpu.HBM)
    smem = pl.BlockSpec(memory_space=pltpu.SMEM)
    vmem = pl.BlockSpec(memory_space=pltpu.VMEM)
    return pl.pallas_call(
        gather_kernel,
        out_shape=(
            pltpu.VMEM((group, units), hidden.dtype),
            pltpu.VMEM((teams, panels, part_rows, picks * BS), out_grad.dtype),
            pltpu.VMEM((picks * per_column, BS, BS), jnp.float32),
            pltpu.SMEM((picks * per_column,), jnp.int32),
        ),
        in_specs=[hbm] * 4,
        out_specs=(vmem, vmem, vmem, smem),
        scratch_shapes=[pltpu.VMEM((group, units), hidden.dtype)] * (teams - 1)
        + [
            pltpu.VMEM((PIECES, piece_rows, column_blocks * BS), out_grad.dtype),
            pltpu.VMEM((PIECES, column_blocks + 1, piece_rows, BS), out_grad.dtype),
            pltpu.VMEM((PIECES, panels, piece_rows, picks * BS), out_grad.dtype),
            pltpu.SMEM(col_owner.shape, jnp.int32),
            pltpu.SMEM(act_rows.shape, jnp.int32),
            pltpu.VMEM((1, lanes), jnp.int32),
            pltpu.SMEM((1, lanes), jnp.int32),
            pltpu.SemaphoreType.REGULAR((max(3, teams - 1) - 1,)),
            pltpu.SemaphoreType.DMA((copies,)),
            pltpu.SemaphoreType.DMA((copies,)),
            pltpu.SemaphoreType.DMA((2 * PIECES + HALVES * teams + 3,)),
        ],
        compiler_params=pltpu.CompilerParams(
            collective_id=0, has_side_effects=True, vmem_limit_bytes=24 << 20
        ),
    )(*(pltpu.with_memory_space_constraint(x, pltpu.HBM) for x in operands))


def finish_kernel(rows_ref, h_ref, g_ref, acc_ref, out_ref, score_ref, buf, ssq, row, sem):
    teams = g_ref.shape[0]
    picks = g_ref.shape[-1] // BS
    slots = buf.shape[0]
    per_column = slots // picks
    shard = shard_of(teams - 1, lax.axis_index("team"), teams)
    ssq[slots:] = jnp.zeros((ssq.shape[0] - slots, BS), jnp.float32)
    copies = []
    for j in range(picks):
        g = g_ref[shard, :, :, j * BS : (j + 1) * BS].reshape(-1, BS)
        for first in range(j * per_column, (j + 1) * per_column, LAST):
            at = slice(first, first + LAST)
            block = acc_ref[at] + products(h_ref, rows_ref, first, LAST, g)
            buf[at] = block
            ssq[at, :] = jnp.sum(block * block, axis=1)
            if (first + LAST) % (per_column // 2) == 0:
                done = pl.ds(first + LAST - per_column // 2, per_column // 2)
                at_sem = sem.at[len(copies)]
                copies.append(pltpu.make_async_copy(buf.at[done], out_ref.at[done], at_sem))
                copies[-1].start()
    total = jnp.sum(ssq[...].T, axis=0, keepdims=True)
    scores = jnp.sqrt(total * (1.0 / (BS * BS)) + epsilon)
    row[...] = scores[:, :slots]
    copies.append(pltpu.make_async_copy(row, score_ref, sem.at[2 * picks]))
    copies[-1].start()
    for copy in copies:
        copy.wait()


def finish(rows, last, grad, acc):
    slots = rows.shape[0]
    picks = grad.shape[-1] // BS
    hbm = pl.BlockSpec(memory_space=pltpu.HBM)
    smem = pl.BlockSpec(memory_space=pltpu.SMEM)
    vmem = pl.BlockSpec(memory_space=pltpu.VMEM)
    return pl.pallas_call(
        finish_kernel,
        out_shape=(
            jax.ShapeDtypeStruct((slots, BS, BS), jnp.float32),
            jax.ShapeDtypeStruct((1, slots), jnp.float32),
        ),
        in_specs=[smem, vmem, vmem, vmem],
        out_specs=(hbm, hbm),
        scratch_shapes=[
            pltpu.VMEM((slots, BS, BS), jnp.float32),
            pltpu.VMEM((pl.cdiv(slots, BS) * BS, BS), jnp.float32),
            pltpu.VMEM((1, slots), jnp.float32),
            pltpu.SemaphoreType.DMA((2 * picks + 1,)),
        ],
        compiler_params=pltpu.CompilerParams(vmem_limit_bytes=20 << 20),
    )(rows, last, grad, acc)


def in_plane(hidden, out_grad, act_rows, col_owner):
    owners_count, cores = lax.axis_size("blk"), lax.axis_size("dp")
    column_blocks = col_owner.shape[0]
    capacity = min(3 * column_blocks // (2 * owners_count), 3 * column_blocks // 4)
    last, grad, acc, rows = gather(
        col_owner,
        jnp.transpose(act_rows, (2, 0, 1)),
        hidden,
        out_grad,
        owners_count * cores,
        capacity // cores,
    )
    gradients, scores = finish(rows, last, grad, acc)
    return (gradients[None, None], scores[None])


def on_device(hidden, out_grad, act_rows, col_owner):
    owners_count = lax.axis_size("blk")
    owner_index = lax.axis_index("blk")
    column_blocks = col_owner.shape[0]
    capacity = min(3 * column_blocks // (2 * owners_count), 3 * column_blocks // 4)
    per_column = act_rows.shape[2]
    owned_all, alive_all = owner_tables(col_owner, owners_count, capacity)
    owned_mine = lax.dynamic_index_in_dim(owned_all, owner_index, 0, keepdims=False)
    alive_mine = lax.dynamic_index_in_dim(alive_all, owner_index, 0, keepdims=False)
    block_rows = jnp.take(act_rows[0], owned_mine, axis=0).reshape(-1)
    grad_full = lax.all_gather(out_grad, "team", axis=1, tiled=True)
    grad_mask = alive_mine.astype(jnp.bfloat16)[None, :, None]
    hidden_piece = lax.all_gather(hidden, "blk", axis=0, tiled=True)
    grad_piece = lax.all_gather(grad_full, "blk", axis=0, tiled=True)
    count_rows = grad_piece.shape[0]
    picked_grad = (
        jnp.take(grad_piece.reshape(count_rows, column_blocks, BS), owned_mine, axis=1) * grad_mask
    )
    hidden_blocks = hidden_piece.reshape(count_rows, -1, BS)
    picked_hidden = jnp.take(hidden_blocks, block_rows, axis=1).reshape(
        count_rows, capacity, per_column, BS
    )
    partial_value = jnp.einsum(
        "ncki,ncj->ckij", picked_hidden, picked_grad, preferred_element_type=jnp.float32
    )
    partial_value = partial_value.reshape(capacity * per_column, BS, BS)
    gradients = lax.psum_scatter(partial_value, "dp", scatter_dimension=0, tiled=True)
    scores = jnp.sqrt(jnp.mean(gradients * gradients, axis=(1, 2)) + epsilon)
    return (gradients[None, None], scores[None, None])


def solution(mesh):
    in_specs = (P(("blk", "dp"), "team"), P(("blk", "dp"), "team"), P("team", None, None), P())
    out_specs = (P("team", "blk", "dp", None, None), P("team", "blk", "dp"))
    square = mesh.shape["blk"] == 4 and mesh.shape["dp"] == 2
    return jax.shard_map(
        in_plane if square else on_device,
        mesh=mesh,
        in_specs=in_specs,
        out_specs=out_specs,
        check_vma=False,
    )
```
